256 devices in a mesh: row: 32 (over z, y), col: 8 (over x, core).
Axes of the slice: x: 4, y: 4, z: 8, core: 2. Of those that a mesh axis runs over, the one named last changes fastest.
Arguments:
- feat_a: bfloat16 [128, 1024, 128], P('row', 'col'), may hold values from -6 to 6
- feat_b: bfloat16 [32, 1024, 128], P('row', 'col'), may hold values from -6 to 6
- conv_weight: bfloat16 [3, 3, 128, 256], replicated, may hold values from -0.1875 to 0.1875
- conv_bias: float32 [256], replicated, may hold values from -3 to 3
- pair_lists: int32 [32, 2], replicated, may hold values from 0 to 7, as said below
- pair_counts: int32 [32], replicated, may hold values from 1 to 2, as said below
Outputs:
- log_conf_a: float32 [128, 1024], P('row', 'col')
- log_col_total: float32 [32, 1024], P('row', 'col')
The draws below stay inside these ranges and needn't reach their ends.
Inputs may be any that keep to these rules, and one draw needn't show every extreme that they name: `pair_lists`: the first pair_counts[r] entries of row r are distinct B blocks; later entries repeat entry 0; every B block is listed by some A block. `pair_counts`: some A block lists 2 B blocks.
All inputs are finite; a program needn't handle non-finite values.
Results may differ from the reference program's by a relative error of at most 0.00037.
Values may be sent and summed in bfloat16 or wider, within the bound.
A program may use at most 64 MiB of HBM per device.

```python
import jax
import jax.numpy as jnp
from jax import lax

CH = 128
DESC = 256
AR = 4
BC = 128
KMAX = 2
HA = 128
WA = 1024
HB = 32
WB = 1024
ABLK = 32
NBLK = 8


def pair_plan(key):
    base = jax.random.fold_in(key, 11)
    key_rotation, key_count = jax.random.split(base)
    rotation = jax.random.randint(key_rotation, (), 0, NBLK)
    firsts = (jnp.arange(ABLK) * NBLK // ABLK + rotation) % NBLK
    counts = jax.random.randint(key_count, (ABLK,), 1, KMAX + 1)
    counts = counts.at[0].set(KMAX)
    offsets = jnp.arange(KMAX)[None, :]
    lists = jnp.where(offsets < counts[:, None], (firsts[:, None] + offsets) % NBLK, firsts[:, None])
    return (lists.astype(jnp.int32), counts.astype(jnp.int32))


def draw_pair_lists(key, part):
    return pair_plan(key)[0]


def draw_pair_counts(key, part):
    return pair_plan(key)[1]


def level_of(rng, dims, cuts, least, largest):
    def one(dim, shards_of):
        steps = jax.random.uniform(jax.random.fold_in(jax.random.fold_in(rng, 6), dim), (shards_of,), jnp.float32, least / len(cuts), largest / len(cuts))
        return jnp.repeat(jnp.exp(steps), dims[dim] // shards_of).reshape((-1,) + (1,) * (len(dims) - dim - 1))

    factor_of = one(*cuts[0])
    for cut in cuts[1:]:
        factor_of = factor_of * one(*cut)
    return factor_of


def centred(stream_key, shape, scale, reach, pieces=(), kind=jnp.bfloat16):
    array = scale * jax.random.normal(stream_key, shape, jnp.float32)
    if pieces:
        array = array * level_of(stream_key, shape, pieces, -0.22, 0.18)
    return jnp.clip(array, -reach, reach).astype(kind)


def setup_inputs(seed: int = 0) -> dict:
    seeds = jax.random.split(jax.random.key(seed), 7)
    feat_a = centred(seeds[0], (HA, WA, CH), 1.0, 6.0, ((0, 32), (1, 8)))
    feat_b = centred(seeds[1], (HB, WB, CH), 1.0, 6.0, ((0, 32), (1, 8)))
    conv_weight = centred(seeds[2], (3, 3, CH, DESC), (9 * CH) ** -0.5, 0.1875)
    conv_bias = centred(seeds[3], (DESC,), 0.5, 3.0, (), jnp.float32)
    pair_lists = draw_pair_lists(jax.random.fold_in(seeds[6], 71), 0)
    pair_counts = draw_pair_counts(jax.random.fold_in(seeds[6], 71), 0)
    return {"feat_a": feat_a, "feat_b": feat_b, "conv_weight": conv_weight, "conv_bias": conv_bias, "pair_lists": pair_lists, "pair_counts": pair_counts}


def describe(features, conv_weight, conv_bias):
    extent_y = features.shape[0]
    extent_x = features.shape[1]
    padded = jnp.pad(features, ((1, 1), (1, 1), (0, 0)))
    total = jnp.zeros((extent_y * extent_x, conv_weight.shape[3]), jnp.float32)
    for i in range(3):
        for j in range(3):
            window = padded[i:i + extent_y, j:j + extent_x].reshape(extent_y * extent_x, features.shape[2])
            total = total + jnp.dot(window, conv_weight[i, j], preferred_element_type=jnp.float32)
    total = total + conv_bias.astype(jnp.float32)[None, :]
    unit = total * lax.rsqrt(lax.optimization_barrier(jnp.mean(total * total, axis=1, keepdims=True)) + 1e-06)
    return unit.astype(jnp.bfloat16)

def reference(feat_a, feat_b, conv_weight, conv_bias, pair_lists, pair_counts):
    unit_a = describe(feat_a, conv_weight, conv_bias).reshape(ABLK, AR * WA, DESC)
    unit_b = describe(feat_b, conv_weight, conv_bias).reshape(HB, NBLK, BC, DESC)
    unit_b = unit_b.transpose(1, 0, 2, 3).reshape(NBLK, HB * BC, DESC)
    score_scale = 1.0 / (DESC * 0.1)

    def scores(block_a, index):
        block_b = lax.dynamic_index_in_dim(unit_b, index, 0, keepdims=False)
        return jnp.dot(block_a.astype(jnp.float32), block_b.astype(jnp.float32).T, precision=lax.Precision.HIGHEST) * score_scale

    def first_pass(col_tot, inputs):
        block_a, listed, live_count = inputs
        row_tot = jnp.zeros((AR * WA,), jnp.float32)
        for k in range(KMAX):
            alive = (k < live_count).astype(jnp.float32)
            weights = jnp.exp(scores(block_a, listed[k])) * alive
            row_tot = row_tot + lax.optimization_barrier(jnp.sum(weights, axis=1))
            current = lax.dynamic_index_in_dim(col_tot, listed[k], 0, keepdims=False)
            col_tot = lax.dynamic_update_index_in_dim(col_tot, current + lax.optimization_barrier(jnp.sum(weights, axis=0)), listed[k], 0)
        return (col_tot, row_tot)
    col_tot, row_tots = lax.scan(first_pass, jnp.zeros((NBLK, HB * BC), jnp.float32), (unit_a, pair_lists, pair_counts))
    log_col = jnp.log(col_tot)

    def second_pass(inputs):
        block_a, listed, live_count, row_tot = inputs
        running = jnp.full((AR * WA,), -jnp.inf, jnp.float32)
        for k in range(KMAX):
            logs = lax.dynamic_index_in_dim(log_col, listed[k], 0, keepdims=False)
            candidate = lax.optimization_barrier(jnp.max(2.0 * scores(block_a, listed[k]) - logs[None, :], axis=1))
            running = jnp.where(k < live_count, jnp.maximum(running, candidate), running)
        return running - jnp.log(row_tot)
    conf = lax.map(second_pass, (unit_a, pair_lists, pair_counts, row_tots)).reshape(HA, WA)
    log_col_total = log_col.reshape(NBLK, HB, BC).transpose(1, 0, 2).reshape(HB, WB)
    return (conf, log_col_total)
```

```python
import functools
import math

import jax
import jax.numpy as jnp
from jax import lax
from jax.experimental import pallas as pl
from jax.experimental.pallas import tpu as pltpu
from jax.sharding import PartitionSpec as P

KMAX = 2
NY = 4
STRIP = 16
MESH = pl.DeviceIdType.MESH
F32 = jnp.float32
BF16 = jnp.bfloat16


def remote(src, dst, send_sem, recv_sem, row, col):
    return pltpu.make_async_remote_copy(
        src_ref=src,
        dst_ref=dst,
        send_sem=send_sem,
        recv_sem=recv_sem,
        device_id=(row, col),
        device_id_type=MESH,
    )


def taps(center, left, right):
    rows, cols, ch = center.shape
    flat = center.reshape(rows * cols, ch)
    place = lax.broadcasted_iota(jnp.int32, center.shape, 1)
    before = pltpu.roll(flat, 1, 0).reshape(center.shape)
    after = pltpu.roll(flat, rows * cols - 1, 0).reshape(center.shape)
    before = jnp.where(place == 0, left, before)
    after = jnp.where(place == cols - 1, right, after)
    return jnp.concatenate(
        [before.astype(BF16), center.astype(BF16), after.astype(BF16)], axis=2
    )


def normalized(total, bias):
    total = total + bias
    mean = jnp.mean(total * total, axis=1, keepdims=True)
    return (total * lax.rsqrt(mean + 1e-06)).astype(BF16)


def kernel(
    n_row, n_col, scale,
    feat_a, feat_b, weight, bias, lists, counts,
    conf_out, logs_out,
    hrow, hcol, brow, unit, ball, taps_a, taps_b, desc_a, desc_b,
    scores, colacc, coly, colz, lchunk, lrecv, logfull,
    rowpart, rowrecv, maxpart, maxrecv,
    halo_s, halo_r, bx_s, bx_r, bz_s, bz_r, by_s, by_r,
    ax_s, ax_r, ap_s, ap_r, cy_s, cy_r, cz_s, cz_r,
    rs_s, rs_r, lg_s, lg_r, mx_s, mx_r,
):
    r = lax.axis_index("row")
    c = lax.axis_index("col")
    nz = n_row // NY
    nx = n_col // 2
    z = r // NY
    y = r % NY
    x = c // 2
    core = c % 2
    up = (r + n_row - 1) % n_row
    down = (r + 1) % n_row
    lf = (c + n_col - 1) % n_col
    rt = (c + 1) % n_col

    def zrow(step):
        return ((z + step) % nz) * NY + y

    def yrow(step):
        return z * NY + (y + step) % NY

    barrier = pltpu.get_barrier_semaphore()
    partners = [(r, (c + s) % n_col) for s in range(1, n_col)]
    partners += [(yrow(s), c) for s in range(1, NY)]
    partners += [(zrow(s), c) for s in range(1, nz)]
    partners += [(v, h) for v in (up, down) for h in (lf, c, rt)]
    for device in partners:
        pl.semaphore_signal(barrier, inc=1, device_id=device, device_id_type=MESH)
    pl.semaphore_wait(barrier, len(partners))

    sends = []

    def go(copy):
        copy.start()
        sends.append(copy)
        return copy

    bx = []
    for s in range(1, n_col):
        bx.append(
            go(remote(feat_b, brow.at[c], bx_s.at[s], bx_r.at[c], r, (c + s) % n_col))
        )
    last = feat_a.shape[1] - STRIP
    edges = [
        (feat_a.at[3], hrow.at[0], down, c),
        (feat_a.at[0], hrow.at[1], up, c),
        (feat_a.at[:, pl.ds(last, STRIP)], hcol.at[0, pl.ds(1, 4)], r, rt),
        (feat_a.at[:, pl.ds(0, STRIP)], hcol.at[1, pl.ds(1, 4)], r, lf),
        (feat_a.at[3, pl.ds(last, STRIP)], hcol.at[0, 0], down, rt),
        (feat_a.at[3, pl.ds(0, STRIP)], hcol.at[1, 0], down, lf),
        (feat_a.at[0, pl.ds(last, STRIP)], hcol.at[0, 5], up, rt),
        (feat_a.at[0, pl.ds(0, STRIP)], hcol.at[1, 5], up, lf),
    ]
    halos = [
        go(remote(src, dst, halo_s.at[i], halo_r.at[i], row, col))
        for i, (src, dst, row, col) in enumerate(edges)
    ]

    brow[c] = feat_b[...]
    for s in range(1, n_col):
        src = (c + n_col - s) % n_col
        remote(feat_b, brow.at[src], bx_s.at[s], bx_r.at[src], r, src).wait_recv()

    strip = pl.ds(pl.multiple_of(c * STRIP, STRIP), STRIP)
    width = feat_b.shape[0]
    unit[pl.ds(0, n_col)] = brow[:, strip, :]
    entry = lax.broadcasted_iota(jnp.int32, (2 * n_col, n_col * width), 0)
    column = lax.broadcasted_iota(jnp.int32, (2 * n_col, n_col * width), 1)
    wanted = jnp.where(
        entry < n_col,
        entry * width + c * STRIP - 1,
        (entry - n_col) * width + c * STRIP + STRIP,
    )
    pick = jnp.where(column == wanted, 1.0, 0.0).astype(BF16)
    row_all = brow[...].reshape(n_col * width, brow.shape[2])
    unit[n_col] = jnp.dot(pick, row_all, preferred_element_type=F32).astype(BF16)

    zs = [4, 3, 5, 2, 6, 1, 7]
    for s in zs:
        go(remote(unit, ball.at[r], bz_s.at[s], bz_r.at[z], zrow(s), c))
    for s in range(1, NY):
        go(remote(unit, ball.at[r], by_s.at[0, s], by_r.at[z, y], yrow(s), c))
    ball[r] = unit[...]

    for i, (src, dst, row, col) in enumerate(edges):
        halos[i].wait_recv()
    zero = jnp.zeros((), F32)
    top = jnp.where(r == 0, zero, hrow[0].astype(F32))
    bottom = jnp.where(r == n_row - 1, zero, hrow[1].astype(F32))
    center = jnp.concatenate([top[None], feat_a[...].astype(F32), bottom[None]], axis=0)
    sixth = lax.broadcasted_iota(jnp.int32, (6, 1, hcol.shape[3]), 0)
    outside = ((sixth == 0) & (r == 0)) | ((sixth == 5) & (r == n_row - 1))
    left = jnp.where(outside | (c == 0), zero, hcol[0].astype(F32)[:, STRIP - 1 : STRIP])
    right = jnp.where(outside | (c == n_col - 1), zero, hcol[1].astype(F32)[:, 0:1])
    taps_a[...] = taps(center, left, right)
    n_a = 4 * feat_a.shape[1]
    total = jnp.zeros((n_a, desc_a.shape[2]), F32)
    for i in range(3):
        window = taps_a[pl.ds(i, 4)].reshape(n_a, taps_a.shape[2])
        total = total + jnp.dot(window, weight[i], preferred_element_type=F32)
    desc_a[c] = normalized(total, bias[...])
    mate = x * 2 + (1 - core)
    for s in (2, 1, 3):
        far = ((x + s) % nx) * 2 + core
        go(remote(desc_a.at[c], desc_a.at[c], ax_s.at[s], ax_r.at[x], r, far))
    go(remote(desc_a.at[c], desc_a.at[c], ap_s.at[0], ap_r.at[x], r, mate))

    for i, s in enumerate((1, 7, 2, 6, 3, 5, 4)):
        src_z = (z + s) % nz
        slot = ball.at[src_z * NY + y]
        remote(unit, slot, bz_s.at[s], bz_r.at[src_z], r, c).wait_recv()
        for t in range(1, NY):
            go(remote(slot, slot, by_s.at[i + 1, t], by_r.at[src_z, y], yrow(t), c))
    for s in (1, 3, 2):
        src_x = (x + s) % nx
        slot = desc_a.at[src_x * 2 + core]
        remote(slot, slot, ax_s.at[s], ax_r.at[src_x], r, c).wait_recv()
        go(remote(slot, slot, ap_s.at[s], ap_r.at[src_x], r, mate))
    for s in (0, 1, 7, 2, 6, 3, 5, 4):
        src_z = (z + s) % nz
        for t in range(1, NY):
            src_y = (y + t) % NY
            slot = ball.at[src_z * NY + src_y]
            remote(slot, slot, by_s.at[0, t], by_r.at[src_z, src_y], r, c).wait_recv()

    listed = [lists[r, k] for k in range(KMAX)]
    live = [counts[r] > k for k in range(KMAX)]
    n_h = n_row
    n_b = n_h * STRIP
    taps_b[0] = jnp.zeros(taps_b.shape[1:], BF16)
    taps_b[n_h + 1] = jnp.zeros(taps_b.shape[1:], BF16)
    beside = ball[:, n_col].astype(F32)
    entry = lax.broadcasted_iota(jnp.int32, beside.shape, 1)
    for k in range(KMAX):
        block = ball[:, listed[k]].astype(F32)
        left = jnp.sum(jnp.where(entry == listed[k], beside, 0.0), axis=1, keepdims=True)
        right = jnp.sum(
            jnp.where(entry == listed[k] + n_col, beside, 0.0), axis=1, keepdims=True
        )
        taps_b[pl.ds(1, n_h)] = taps(block, left, right)
        total = jnp.zeros((n_b, desc_b.shape[2]), F32)
        for i in range(3):
            window = taps_b[pl.ds(i, n_h)].reshape(n_b, taps_b.shape[2])
            total = total + jnp.dot(window, weight[i], preferred_element_type=F32)
        desc_b[k] = normalized(total, bias[...])

    for s in range(nx):
        src_x = (x + s) % nx
        slot = desc_a.at[src_x * 2 + (1 - core)]
        remote(slot, slot, ap_s.at[s], ap_r.at[src_x], r, c).wait_recv()

    colacc[...] = jnp.zeros(colacc.shape, F32)
    groups = n_a // 128
    to_exp2 = scale * math.log2(math.e)

    def first(j, carry):
        cells = desc_a[j]
        rows = [jnp.zeros((1, 128), F32) for _ in range(groups)]
        for k in range(KMAX):
            found = lax.dot_general(
                desc_b[k], cells, (((1,), (1,)), ((), ())), preferred_element_type=F32
            )
            scores[k, j] = found
            acc = jnp.zeros((n_b, 128), F32)
            for g in range(groups):
                weights = jnp.exp2(found[:, g * 128 : (g + 1) * 128] * to_exp2)
                acc = acc + weights
                part = jnp.sum(weights, axis=0, keepdims=True)
                rows[g] = rows[g] + jnp.where(live[k], part, 0.0)
            colacc[k] = colacc[k] + acc
        rowpart[j] = jnp.concatenate(rows + rows, axis=0)
        return carry

    lax.fori_loop(0, n_col, first, 0)

    which = lax.broadcasted_iota(jnp.int32, (n_col, n_b), 0)
    own = jnp.zeros((n_col, n_b), F32)
    for k in range(KMAX):
        line = jnp.sum(colacc[k].T, axis=0, keepdims=True)
        own = own + jnp.where((which == listed[k]) & live[k], line, 0.0)
    coly[y] = own
    for s in (2, 1, 3):
        go(remote(coly.at[y], coly.at[y], cy_s.at[s], cy_r.at[y], yrow(s), c))
    for s in range(1, n_col):
        far = (c + s) % n_col
        go(remote(rowpart.at[far], rowrecv.at[c], rs_s.at[s], rs_r.at[c], r, far))
    rowrecv[c] = rowpart[c]
    for s in (1, 3, 2):
        src = (y + s) % NY
        slot = coly.at[src]
        remote(slot, slot, cy_s.at[s], cy_r.at[src], r, c).wait_recv()
    colz[z] = jnp.sum(coly[...], axis=0)
    for s in zs:
        go(remote(colz.at[z], colz.at[z], cz_s.at[s], cz_r.at[z], zrow(s), c))
    for s in (1, 7, 2, 6, 3, 5, 4):
        src = (z + s) % nz
        slot = colz.at[src]
        remote(slot, slot, cz_s.at[s], cz_r.at[src], r, c).wait_recv()
    logs = jnp.log(jnp.sum(colz[...], axis=0))
    logfull[...] = logs
    per = 128 // STRIP
    chunk = pl.ds(pl.multiple_of((r // per) * 128, 128), 128)
    lchunk[...] = logfull[:, chunk]
    lrecv[c] = lchunk[...]
    for s in range(1, n_col):
        far = (c + s) % n_col
        go(remote(lchunk, lrecv.at[c], lg_s.at[s], lg_r.at[c], r, far))

    lower = []
    for k in range(KMAX):
        line = jnp.sum(jnp.where(which == listed[k], logs, 0.0), axis=0, keepdims=True)
        lower.append(jnp.broadcast_to(line * (0.5 / scale), (128, n_b)).T)
    for k in range(KMAX):
        colacc[k] = lower[k]

    def second(j, carry):
        best = [jnp.full((1, 128), -jnp.inf, F32) for _ in range(groups)]
        for k in range(KMAX):
            for g in range(groups):
                candidate = scores[k, j, :, pl.ds(g * 128, 128)] - colacc[k]
                top_of = jnp.max(candidate, axis=0, keepdims=True)
                best[g] = jnp.maximum(best[g], jnp.where(live[k], top_of, -jnp.inf))
        maxpart[j] = jnp.concatenate(best + best, axis=0)
        return carry

    lax.fori_loop(0, n_col, second, 0)
    for s in range(1, n_col):
        far = (c + s) % n_col
        go(remote(maxpart.at[far], maxrecv.at[c], mx_s.at[s], mx_r.at[c], r, far))
    maxrecv[c] = maxpart[c]

    for s in range(1, n_col):
        src = (c + n_col - s) % n_col
        remote(rowpart.at[src], rowrecv.at[src], rs_s.at[s], rs_r.at[src], r, c).wait_recv()
        remote(lchunk, lrecv.at[src], lg_s.at[s], lg_r.at[src], r, c).wait_recv()
    row_log = jnp.log(jnp.sum(rowrecv[...], axis=0))
    lane = lax.broadcasted_iota(jnp.int32, (n_col, 128), 1)
    sub = lax.broadcasted_iota(jnp.int32, (n_col, 128), 0)
    out = jnp.zeros((n_col, 128), F32)
    for j in range(n_col):
        shift = (STRIP * j + 128 - STRIP * (r % per)) % 128
        moved = pltpu.roll(lrecv[j], shift, 1)
        out = out + jnp.where((lane // STRIP == j) & (sub == c), moved, 0.0)
    logs_out[...] = jnp.sum(out, axis=0, keepdims=True)
    for s in range(1, n_col):
        src = (c + n_col - s) % n_col
        remote(maxpart.at[src], maxrecv.at[src], mx_s.at[s], mx_r.at[src], r, c).wait_recv()
    best = jnp.max(maxrecv[...], axis=0) * (2.0 * scale) - row_log
    conf_out[...] = best[0:4]
    for copy in sends:
        copy.wait_send()


def local(feat_a, feat_b, conv_weight, conv_bias, pair_lists, pair_counts):
    n_row = lax.axis_size("row")
    n_col = lax.axis_size("col")
    ch = feat_a.shape[2]
    width = feat_a.shape[1]
    desc = conv_weight.shape[3]
    n_a = feat_a.shape[0] * width
    n_b = n_row * STRIP
    nz = n_row // NY
    nx = n_col // 2
    scale = 1.0 / (desc * 0.1)
    vmem = pl.BlockSpec(memory_space=pltpu.VMEM)
    smem = pl.BlockSpec(memory_space=pltpu.SMEM)
    dma = pltpu.SemaphoreType.DMA
    scratch = [
        pltpu.VMEM((2, width, ch), BF16),
        pltpu.VMEM((2, 6, STRIP, ch), BF16),
        pltpu.VMEM((n_col, width, ch), BF16),
        pltpu.VMEM((n_col + 1, STRIP, ch), BF16),
        pltpu.VMEM((n_row, n_col + 1, STRIP, ch), BF16),
        pltpu.VMEM((6, width, 3 * ch), BF16),
        pltpu.VMEM((n_row + 2, STRIP, 3 * ch), BF16),
        pltpu.VMEM((n_col, n_a, desc), BF16),
        pltpu.VMEM((KMAX, n_b, desc), BF16),
        pltpu.VMEM((KMAX, n_col, n_b, n_a), F32),
        pltpu.VMEM((KMAX, n_b, 128), F32),
        pltpu.VMEM((NY, n_col, n_b), F32),
        pltpu.VMEM((nz, n_col, n_b), F32),
        pltpu.VMEM((n_col, 128), F32),
        pltpu.VMEM((n_col, n_col, 128), F32),
        pltpu.VMEM((n_col, n_b), F32),
    ]
    scratch += [pltpu.VMEM((n_col, 8, 128), F32)] * 4
    for shape in (
        (8,), (n_col,), (nz,), (nz, NY), (nx,), (nx,), (NY,), (nz,),
        (n_col,), (n_col,), (n_col,),
    ):
        received = (nz, NY) if shape == (nz, NY) else shape
        scratch += [dma(shape), dma(received)]
    run = pl.pallas_call(
        functools.partial(kernel, n_row, n_col, scale),
        out_shape=(
            jax.ShapeDtypeStruct((4, 128), F32),
            jax.ShapeDtypeStruct((1, 128), F32),
        ),
        in_specs=[vmem, vmem, vmem, vmem, smem, smem],
        out_specs=(vmem, vmem),
        scratch_shapes=scratch,
        compiler_params=pltpu.CompilerParams(
            collective_id=0, has_side_effects=True, vmem_limit_bytes=56 * 1024 * 1024
        ),
    )
    conf, logs = run(
        feat_a,
        feat_b.reshape(feat_b.shape[1], ch),
        conv_weight.reshape(3, 3 * ch, desc),
        conv_bias.reshape(1, desc),
        pair_lists,
        pair_counts,
    )
    return (conf, logs)


def solution(mesh):
    in_specs = (P("row", "col", None), P("row", "col", None), P(), P(), P(), P())
    out_specs = (P("row", "col"), P("row", "col"))
    return jax.shard_map(local, mesh=mesh, in_specs=in_specs, out_specs=out_specs, check_vma=False)
```

```python
import functools
import math

import jax
import jax.numpy as jnp
from jax import lax
from jax.experimental import pallas as pl
from jax.experimental.pallas import tpu as pltpu
from jax.sharding import PartitionSpec as P

KMAX = 2
NY = 4
STRIP = 16
MESH = pl.DeviceIdType.MESH
F32 = jnp.float32
BF16 = jnp.bfloat16


def remote(src, dst, send_sem, recv_sem, row, col):
    return pltpu.make_async_remote_copy(
        src_ref=src,
        dst_ref=dst,
        send_sem=send_sem,
        recv_sem=recv_sem,
        device_id=(row, col),
        device_id_type=MESH,
    )


def taps(center, left, right):
    rows, cols, ch = center.shape
    flat = center.reshape(rows * cols, ch)
    place = lax.broadcasted_iota(jnp.int32, center.shape, 1)
    before = pltpu.roll(flat, 1, 0).reshape(center.shape)
    after = pltpu.roll(flat, rows * cols - 1, 0).reshape(center.shape)
    before = jnp.where(place == 0, left, before)
    after = jnp.where(place == cols - 1, right, after)
    return jnp.concatenate(
        [before.astype(BF16), center.astype(BF16), after.astype(BF16)], axis=2
    )


def normalized(total, bias):
    total = total + bias
    mean = jnp.mean(total * total, axis=1, keepdims=True)
    return (total * lax.rsqrt(mean + 1e-06)).astype(BF16)


def kernel(
    n_row, n_col, scale,
    feat_a_in, feat_b_in, weight_in, bias_in, lists, counts,
    conf_out, logs_out,
    feat_a, tiles, weight, bias, hrow, hcol, brow, unit, ball, taps_a, taps_b, desc_a, desc_b,
    scores, colacc, coly, colz, lchunk, lrecv, logfull,
    rowpart, rowrecv, maxpart, maxrecv,
    halo_s, halo_r, bx_s, bx_r, bz_s, bz_r, by_s, by_r,
    ax_s, ax_r, ap_s, ap_r, cy_s, cy_r, cz_s, cz_r,
    rs_s, rs_r, lg_s, lg_r, mx_s, mx_r, in_sem,
):
    r = lax.axis_index("row")
    c = lax.axis_index("col")
    nz = n_row // NY
    nx = n_col // 2
    z = r // NY
    y = r % NY
    x = c // 2
    core = c % 2
    up = (r + n_row - 1) % n_row
    down = (r + 1) % n_row
    lf = (c + n_col - 1) % n_col
    rt = (c + 1) % n_col

    def zrow(step):
        return ((z + step) % nz) * NY + y

    def yrow(step):
        return z * NY + (y + step) % NY

    tail = pl.ds(n_col - 1, 1)
    fetches = [
        pltpu.make_async_copy(src, dst, in_sem.at[i])
        for i, (src, dst) in enumerate(
            [
                (feat_b_in, tiles.at[pl.ds(1, n_col)]),
                (feat_b_in.at[tail], tiles.at[pl.ds(0, 1)]),
                (feat_b_in.at[pl.ds(0, 1)], tiles.at[pl.ds(n_col + 1, 1)]),
                (feat_a_in, feat_a),
                (weight_in, weight),
                (bias_in, bias),
            ]
        )
    ]
    for fetch in fetches:
        fetch.start()
    barrier = pltpu.get_barrier_semaphore()
    partners = [(r, (c + s) % n_col) for s in range(1, n_col)]
    partners += [(yrow(s), c) for s in range(1, NY)]
    partners += [(zrow(s), c) for s in range(1, nz)]
    partners += [(v, h) for v in (up, down) for h in (lf, c, rt)]
    for device in partners:
        pl.semaphore_signal(barrier, inc=1, device_id=device, device_id_type=MESH)
    pl.semaphore_wait(barrier, len(partners))

    sends = []

    def go(copy):
        copy.start()
        sends.append(copy)
        return copy

    for fetch in fetches[:3]:
        fetch.wait()
    brow[c] = tiles[pl.ds(c, 3)]
    for s in range(1, n_col):
        far = (c + s) % n_col
        go(remote(tiles.at[pl.ds(far, 3)], brow.at[c], bx_s.at[s], bx_r.at[c], r, far))
    last = feat_a.shape[1] - STRIP
    edges = [
        (feat_a_in.at[3], hrow.at[0], down, c),
        (feat_a_in.at[0], hrow.at[1], up, c),
        (feat_a_in.at[:, pl.ds(last, STRIP)], hcol.at[0, pl.ds(1, 4)], r, rt),
        (feat_a_in.at[:, pl.ds(0, STRIP)], hcol.at[1, pl.ds(1, 4)], r, lf),
        (feat_a_in.at[3, pl.ds(last, STRIP)], hcol.at[0, 0], down, rt),
        (feat_a_in.at[3, pl.ds(0, STRIP)], hcol.at[1, 0], down, lf),
        (feat_a_in.at[0, pl.ds(last, STRIP)], hcol.at[0, 5], up, rt),
        (feat_a_in.at[0, pl.ds(0, STRIP)], hcol.at[1, 5], up, lf),
    ]
    halos = [
        go(remote(src, dst, halo_s.at[i], halo_r.at[i], row, col))
        for i, (src, dst, row, col) in enumerate(edges)
    ]

    for s in range(1, n_col):
        src = (c + n_col - s) % n_col
        mine = brow.at[src]
        remote(mine, mine, bx_s.at[s], bx_r.at[src], r, src).wait_recv()

    unit[pl.ds(0, n_col)] = brow[:, 1]
    entry = lax.broadcasted_iota(jnp.int32, (2 * n_col, n_col * 3 * STRIP), 0)
    column = lax.broadcasted_iota(jnp.int32, (2 * n_col, n_col * 3 * STRIP), 1)
    at_start = jnp.where(c == 0, 1, 0)
    at_end = jnp.where(c == n_col - 1, 1, 0)
    wanted = jnp.where(
        entry < n_col,
        (entry - at_start) * 3 * STRIP + STRIP - 1,
        (entry - n_col + at_end) * 3 * STRIP + 2 * STRIP,
    )
    pick = jnp.where(column == wanted, 1.0, 0.0).astype(BF16)
    row_all = brow[...].reshape(n_col * 3 * STRIP, brow.shape[3])
    unit[n_col] = jnp.dot(pick, row_all, preferred_element_type=F32).astype(BF16)

    d = 1 - 2 * core
    zup, zdown, yup, ydown = zrow(1), zrow(nz - 1), yrow(1), yrow(NY - 1)
    own = ball.at[r]
    go(remote(unit, own, bz_s.at[0, 0], bz_r.at[z], zup, c))
    go(remote(unit, own, bz_s.at[1, 0], bz_r.at[z], zdown, c))
    go(remote(unit, own, by_s.at[0, z], by_r.at[z, y], yup, c))
    go(remote(unit, own, by_s.at[1, z], by_r.at[z, y], ydown, c))
    ball[r] = unit[...]

    def z_arrived(step):
        src_z = (z + step + nz) % nz
        slot = ball.at[src_z * NY + y]
        remote(slot, slot, bz_s.at[0, 0], bz_r.at[src_z], r, c).wait_recv()
        return src_z, slot

    def z_forward(slot, src_z, way, to, hop):
        go(remote(slot, slot, bz_s.at[way, hop], bz_r.at[src_z], to, c))

    def y_forward(slot, src_z):
        go(remote(slot, slot, by_s.at[0, src_z], by_r.at[src_z, y], yup, c))
        go(remote(slot, slot, by_s.at[1, src_z], by_r.at[src_z, y], ydown, c))

    def y_arrived(step, src_y):
        src_z = (z + step + nz) % nz
        slot = ball.at[src_z * NY + src_y]
        remote(slot, slot, by_s.at[0, 0], by_r.at[src_z, src_y], r, c).wait_recv()
        return src_z, slot

    def y_relay(step):
        src_y = (y - d + NY) % NY
        src_z, slot = y_arrived(step, src_y)
        to = z * NY + (y + d + NY) % NY
        go(remote(slot, slot, by_s.at[2, src_z], by_r.at[src_z, src_y], to, c))

    fetches[3].wait()
    fetches[4].wait()
    fetches[5].wait()
    for i, (src, dst, row, col) in enumerate(edges):
        halos[i].wait_recv()
    zero = jnp.zeros((), F32)
    top = jnp.where(r == 0, zero, hrow[0].astype(F32))
    bottom = jnp.where(r == n_row - 1, zero, hrow[1].astype(F32))
    center = jnp.concatenate([top[None], feat_a[...].astype(F32), bottom[None]], axis=0)
    sixth = lax.broadcasted_iota(jnp.int32, (6, 1, hcol.shape[3]), 0)
    outside = ((sixth == 0) & (r == 0)) | ((sixth == 5) & (r == n_row - 1))
    left = jnp.where(outside | (c == 0), zero, hcol[0].astype(F32)[:, STRIP - 1 : STRIP])
    right = jnp.where(outside | (c == n_col - 1), zero, hcol[1].astype(F32)[:, 0:1])
    taps_a[...] = taps(center, left, right)
    n_a = 4 * feat_a.shape[1]
    total = jnp.zeros((n_a, desc_a.shape[2]), F32)
    for i in range(3):
        window = taps_a[pl.ds(i, 4)].reshape(n_a, taps_a.shape[2])
        total = total + jnp.dot(window, weight[i], preferred_element_type=F32)
    desc_a[c] = normalized(total, bias[...])
    mate = x * 2 + (1 - core)
    mine = desc_a.at[c]
    xup = ((x + 1) % nx) * 2 + core
    xdown = ((x + nx - 1) % nx) * 2 + core
    xnext = ((x + d + nx) % nx) * 2 + core
    go(remote(mine, mine, ax_s.at[0], ax_r.at[x], r, xup))
    go(remote(mine, mine, ax_s.at[1], ax_r.at[x], r, xdown))
    go(remote(mine, mine, ap_s.at[0], ap_r.at[x], r, mate))

    def x_arrived(step, hop):
        src_x = (x + step + nx) % nx
        slot = desc_a.at[src_x * 2 + core]
        remote(slot, slot, ax_s.at[0], ax_r.at[src_x], r, c).wait_recv()
        if hop == 1:
            go(remote(slot, slot, ax_s.at[2], ax_r.at[src_x], r, xnext))
        go(remote(slot, slot, ap_s.at[hop], ap_r.at[src_x], r, mate))

    for hop in (1, 2):
        for way, step, to in ((0, -hop, zup), (1, hop, zdown)):
            src_z, slot = z_arrived(step)
            z_forward(slot, src_z, way, to, hop)
            y_forward(slot, src_z)
        if hop == 1:
            y_relay(0)
        else:
            y_relay(-1)
            y_relay(1)
    z_up = (z + d + nz) % nz
    src_z, slot = z_arrived(-3 * d)
    z_forward(slot, src_z, 0, z_up * NY + y, 3)
    y_forward(slot, src_z)
    src_z, slot = z_arrived(3 * d)
    y_forward(slot, src_z)
    x_arrived(-d, 1)
    y_relay(-2)
    y_relay(2)
    x_arrived(d, 2)
    src_z, slot = z_arrived(4)
    y_forward(slot, src_z)
    y_relay(-3)
    y_relay(3)
    y_relay(4)
    x_arrived(2, 3)
    for step in (0, -1, 1, -2, 2, -3, 3, 4):
        y_arrived(step, (y + d + NY) % NY)
        y_arrived(step, (y + 2) % NY)

    listed = [lists[r, k] for k in range(KMAX)]
    live = [counts[r] > k for k in range(KMAX)]
    n_h = n_row
    n_b = n_h * STRIP
    taps_b[0] = jnp.zeros(taps_b.shape[1:], BF16)
    taps_b[n_h + 1] = jnp.zeros(taps_b.shape[1:], BF16)
    beside = ball[:, n_col].astype(F32)
    entry = lax.broadcasted_iota(jnp.int32, beside.shape, 1)
    for k in range(KMAX):
        block = ball[:, listed[k]].astype(F32)
        left = jnp.sum(jnp.where(entry == listed[k], beside, 0.0), axis=1, keepdims=True)
        right = jnp.sum(
            jnp.where(entry == listed[k] + n_col, beside, 0.0), axis=1, keepdims=True
        )
        taps_b[pl.ds(1, n_h)] = taps(block, left, right)
        total = jnp.zeros((n_b, desc_b.shape[2]), F32)
        for i in range(3):
            window = taps_b[pl.ds(i, n_h)].reshape(n_b, taps_b.shape[2])
            total = total + jnp.dot(window, weight[i], preferred_element_type=F32)
        desc_b[k] = normalized(total, bias[...])

    for s in range(nx):
        src_x = (x + s) % nx
        slot = desc_a.at[src_x * 2 + (1 - core)]
        remote(slot, slot, ap_s.at[s], ap_r.at[src_x], r, c).wait_recv()

    colacc[...] = jnp.zeros(colacc.shape, F32)
    groups = n_a // 128
    to_exp2 = scale * math.log2(math.e)

    def first(j, carry):
        cells = desc_a[j]
        rows = [jnp.zeros((1, 128), F32) for _ in range(groups)]
        for k in range(KMAX):
            found = lax.dot_general(
                desc_b[k], cells, (((1,), (1,)), ((), ())), preferred_element_type=F32
            )
            scores[k, j] = found
            acc = jnp.zeros((n_b, 128), F32)
            for g in range(groups):
                weights = jnp.exp2(found[:, g * 128 : (g + 1) * 128] * to_exp2)
                acc = acc + weights
                part = jnp.sum(weights, axis=0, keepdims=True)
                rows[g] = rows[g] + jnp.where(live[k], part, 0.0)
            colacc[k] = colacc[k] + acc
        rowpart[j] = jnp.concatenate(rows + rows, axis=0)
        return carry

    lax.fori_loop(0, n_col, first, 0)

    which = lax.broadcasted_iota(jnp.int32, (n_col, n_b), 0)
    own = jnp.zeros((n_col, n_b), F32)
    for k in range(KMAX):
        line = jnp.sum(colacc[k].T, axis=0, keepdims=True)
        own = own + jnp.where((which == listed[k]) & live[k], line, 0.0)
    coly[y] = own
    for s in (2, 1, 3):
        go(remote(coly.at[y], coly.at[y], cy_s.at[s], cy_r.at[y], yrow(s), c))
    for s in range(1, n_col):
        far = (c + s) % n_col
        go(remote(rowpart.at[far], rowrecv.at[c], rs_s.at[s], rs_r.at[c], r, far))
    rowrecv[c] = rowpart[c]
    for s in (1, 3, 2):
        src = (y + s) % NY
        slot = coly.at[src]
        remote(slot, slot, cy_s.at[s], cy_r.at[src], r, c).wait_recv()
    colz[z] = jnp.sum(coly[...], axis=0)
    for s in (4, 3, 5, 2, 6, 1, 7):
        go(remote(colz.at[z], colz.at[z], cz_s.at[s], cz_r.at[z], zrow(s), c))
    for s in (1, 7, 2, 6, 3, 5, 4):
        src = (z + s) % nz
        slot = colz.at[src]
        remote(slot, slot, cz_s.at[s], cz_r.at[src], r, c).wait_recv()
    logs = jnp.log(jnp.sum(colz[...], axis=0))
    logfull[...] = logs
    per = 128 // STRIP
    chunk = pl.ds(pl.multiple_of((r // per) * 128, 128), 128)
    lchunk[...] = logfull[:, chunk]
    lrecv[c] = lchunk[...]
    for s in range(1, n_col):
        far = (c + s) % n_col
        go(remote(lchunk, lrecv.at[c], lg_s.at[s], lg_r.at[c], r, far))

    lower = []
    for k in range(KMAX):
        line = jnp.sum(jnp.where(which == listed[k], logs, 0.0), axis=0, keepdims=True)
        lower.append(jnp.broadcast_to(line * (0.5 / scale), (128, n_b)).T)
    for k in range(KMAX):
        colacc[k] = lower[k]

    def second(j, carry):
        best = [jnp.full((1, 128), -jnp.inf, F32) for _ in range(groups)]
        for k in range(KMAX):
            for g in range(groups):
                candidate = scores[k, j, :, pl.ds(g * 128, 128)] - colacc[k]
                top_of = jnp.max(candidate, axis=0, keepdims=True)
                best[g] = jnp.maximum(best[g], jnp.where(live[k], top_of, -jnp.inf))
        maxpart[j] = jnp.concatenate(best + best, axis=0)
        return carry

    lax.fori_loop(0, n_col, second, 0)
    for s in range(1, n_col):
        far = (c + s) % n_col
        go(remote(maxpart.at[far], maxrecv.at[c], mx_s.at[s], mx_r.at[c], r, far))
    maxrecv[c] = maxpart[c]

    for s in range(1, n_col):
        src = (c + n_col - s) % n_col
        remote(rowpart.at[src], rowrecv.at[src], rs_s.at[s], rs_r.at[src], r, c).wait_recv()
        remote(lchunk, lrecv.at[src], lg_s.at[s], lg_r.at[src], r, c).wait_recv()
    row_log = jnp.log(jnp.sum(rowrecv[...], axis=0))
    lane = lax.broadcasted_iota(jnp.int32, (n_col, 128), 1)
    sub = lax.broadcasted_iota(jnp.int32, (n_col, 128), 0)
    out = jnp.zeros((n_col, 128), F32)
    for j in range(n_col):
        shift = (STRIP * j + 128 - STRIP * (r % per)) % 128
        moved = pltpu.roll(lrecv[j], shift, 1)
        out = out + jnp.where((lane // STRIP == j) & (sub == c), moved, 0.0)
    logs_out[...] = jnp.sum(out, axis=0, keepdims=True)
    for s in range(1, n_col):
        src = (c + n_col - s) % n_col
        remote(maxpart.at[src], maxrecv.at[src], mx_s.at[s], mx_r.at[src], r, c).wait_recv()
    best = jnp.max(maxrecv[...], axis=0) * (2.0 * scale) - row_log
    conf_out[...] = best[0:4]
    for copy in sends:
        copy.wait_send()


def local(feat_a, feat_b, conv_weight, conv_bias, pair_lists, pair_counts):
    n_row = lax.axis_size("row")
    n_col = lax.axis_size("col")
    ch = feat_a.shape[2]
    width = feat_a.shape[1]
    desc = conv_weight.shape[3]
    n_a = feat_a.shape[0] * width
    n_b = n_row * STRIP
    nz = n_row // NY
    nx = n_col // 2
    scale = 1.0 / (desc * 0.1)
    vmem = pl.BlockSpec(memory_space=pltpu.VMEM)
    hbm = pl.BlockSpec(memory_space=pl.ANY)
    smem = pl.BlockSpec(memory_space=pltpu.SMEM)
    dma = pltpu.SemaphoreType.DMA
    scratch = [
        pltpu.VMEM(feat_a.shape, BF16),
        pltpu.VMEM((n_col + 2, STRIP, ch), BF16),
        pltpu.VMEM((3, 3 * ch, desc), BF16),
        pltpu.VMEM((1, desc), F32),
        pltpu.VMEM((2, width, ch), BF16),
        pltpu.VMEM((2, 6, STRIP, ch), BF16),
        pltpu.VMEM((n_col, 3, STRIP, ch), BF16),
        pltpu.VMEM((n_col + 1, STRIP, ch), BF16),
        pltpu.VMEM((n_row, n_col + 1, STRIP, ch), BF16),
        pltpu.VMEM((6, width, 3 * ch), BF16),
        pltpu.VMEM((n_row + 2, STRIP, 3 * ch), BF16),
        pltpu.VMEM((n_col, n_a, desc), BF16),
        pltpu.VMEM((KMAX, n_b, desc), BF16),
        pltpu.VMEM((KMAX, n_col, n_b, n_a), F32),
        pltpu.VMEM((KMAX, n_b, 128), F32),
        pltpu.VMEM((NY, n_col, n_b), F32),
        pltpu.VMEM((nz, n_col, n_b), F32),
        pltpu.VMEM((n_col, 128), F32),
        pltpu.VMEM((n_col, n_col, 128), F32),
        pltpu.VMEM((n_col, n_b), F32),
    ]
    scratch += [pltpu.VMEM((n_col, 8, 128), F32)] * 4
    for sent, received in (
        ((8,), (8,)),
        ((n_col,), (n_col,)),
        ((2, 4), (nz,)),
        ((3, nz), (nz, NY)),
        ((3,), (nx,)),
        ((nx,), (nx,)),
        ((NY,), (NY,)),
        ((nz,), (nz,)),
        ((n_col,), (n_col,)),
        ((n_col,), (n_col,)),
        ((n_col,), (n_col,)),
    ):
        scratch += [dma(sent), dma(received)]
    scratch.append(dma((6,)))
    run = pl.pallas_call(
        functools.partial(kernel, n_row, n_col, scale),
        out_shape=(
            jax.ShapeDtypeStruct((4, 128), F32),
            jax.ShapeDtypeStruct((1, 128), F32),
        ),
        in_specs=[hbm, hbm, hbm, hbm, smem, smem],
        out_specs=(vmem, vmem),
        scratch_shapes=scratch,
        compiler_params=pltpu.CompilerParams(
            collective_id=0, has_side_effects=True, vmem_limit_bytes=56 * 1024 * 1024
        ),
    )
    conf, logs = run(
        feat_a,
        feat_b.reshape(width // STRIP, STRIP, ch),
        conv_weight.reshape(3, 3 * ch, desc),
        conv_bias.reshape(1, desc),
        pair_lists,
        pair_counts,
    )
    return (conf, logs)


def solution(mesh):
    in_specs = (P("row", "col", None), P("row", "col", None), P(), P(), P(), P())
    out_specs = (P("row", "col"), P("row", "col"))
    return jax.shard_map(local, mesh=mesh, in_specs=in_specs, out_specs=out_specs, check_vma=False)
```

```python
import functools
import math

import jax
import jax.numpy as jnp
from jax import lax
from jax.experimental import pallas as pl
from jax.experimental.pallas import tpu as pltpu
from jax.sharding import PartitionSpec as P

KMAX = 2
NY = 4
STRIP = 16
MESH = pl.DeviceIdType.MESH
F32 = jnp.float32
BF16 = jnp.bfloat16


def remote(src, dst, send_sem, recv_sem, row, col):
    return pltpu.make_async_remote_copy(
        src_ref=src,
        dst_ref=dst,
        send_sem=send_sem,
        recv_sem=recv_sem,
        device_id=(row, col),
        device_id_type=MESH,
    )


def taps(center, left, right):
    rows, cols, ch = center.shape
    flat = center.reshape(rows * cols, ch)
    place = lax.broadcasted_iota(jnp.int32, center.shape, 1)
    before = pltpu.roll(flat, 1, 0).reshape(center.shape)
    after = pltpu.roll(flat, rows * cols - 1, 0).reshape(center.shape)
    before = jnp.where(place == 0, left, before)
    after = jnp.where(place == cols - 1, right, after)
    return jnp.concatenate(
        [before.astype(BF16), center.astype(BF16), after.astype(BF16)], axis=2
    )


def normalized(total, bias):
    total = total + bias
    mean = jnp.mean(total * total, axis=1, keepdims=True)
    return (total * lax.rsqrt(mean + 1e-06)).astype(BF16)


def kernel(
    n_row, n_col, scale,
    feat_a_in, feat_b_in, weight_in, bias_in, lists, counts,
    out_ref,
    feat_a, tiles, weight, bias, hrow, hcol, brow, unit, ball, taps_a, taps_b, desc_a, desc_b,
    scores, colacc, colown, coly, colz, lchunk, lrecv, logfull,
    rowpart, rowrecv, maxpart, maxrecv,
    halo_s, halo_r, bx_s, bx_r, bz_s, bz_r, by_s, by_r,
    ax_s, ax_r, ap_s, ap_r, cy_s, cy_r, cz_s, cz_r,
    rs_s, rs_r, lg_s, lg_r, mx_s, mx_r, cl_s, cl_r, in_sem,
):
    r = lax.axis_index("row")
    c = lax.axis_index("col")
    nz = n_row // NY
    nx = n_col // 2
    z = r // NY
    y = r % NY
    x = c // 2
    core = c % 2
    up = (r + n_row - 1) % n_row
    down = (r + 1) % n_row
    lf = (c + n_col - 1) % n_col
    rt = (c + 1) % n_col

    def zrow(step):
        return ((z + step) % nz) * NY + y

    def yrow(step):
        return z * NY + (y + step) % NY

    tail = pl.ds(n_col - 1, 1)
    fetches = [
        pltpu.make_async_copy(src, dst, in_sem.at[i])
        for i, (src, dst) in enumerate(
            [
                (feat_b_in, tiles.at[pl.ds(1, n_col)]),
                (feat_b_in.at[tail], tiles.at[pl.ds(0, 1)]),
                (feat_b_in.at[pl.ds(0, 1)], tiles.at[pl.ds(n_col + 1, 1)]),
                (feat_a_in, feat_a),
                (weight_in, weight),
                (bias_in, bias),
            ]
        )
    ]
    for fetch in fetches:
        fetch.start()
    barrier = pltpu.get_barrier_semaphore()
    partners = [(r, (c + s) % n_col) for s in range(1, n_col)]
    partners += [(yrow(1), c), (yrow(NY - 1), c), (zrow(1), c), (zrow(nz - 1), c)]
    partners += [(v, h) for v in (up, down) for h in (lf, c, rt)]
    for device in partners:
        pl.semaphore_signal(barrier, inc=1, device_id=device, device_id_type=MESH)
    pl.semaphore_wait(barrier, len(partners))

    sends = []

    def go(copy):
        copy.start()
        sends.append(copy)
        return copy

    for fetch in fetches[:3]:
        fetch.wait()
    brow[c] = tiles[pl.ds(c, 3)]
    for s in range(1, n_col):
        far = (c + s) % n_col
        go(remote(tiles.at[pl.ds(far, 3)], brow.at[c], bx_s.at[s], bx_r.at[c], r, far))
    last = feat_a.shape[1] - STRIP
    edges = [
        (feat_a_in.at[3], hrow.at[0], down, c),
        (feat_a_in.at[0], hrow.at[1], up, c),
        (feat_a_in.at[:, pl.ds(last, STRIP)], hcol.at[0, pl.ds(1, 4)], r, rt),
        (feat_a_in.at[:, pl.ds(0, STRIP)], hcol.at[1, pl.ds(1, 4)], r, lf),
        (feat_a_in.at[3, pl.ds(last, STRIP)], hcol.at[0, 0], down, rt),
        (feat_a_in.at[3, pl.ds(0, STRIP)], hcol.at[1, 0], down, lf),
        (feat_a_in.at[0, pl.ds(last, STRIP)], hcol.at[0, 5], up, rt),
        (feat_a_in.at[0, pl.ds(0, STRIP)], hcol.at[1, 5], up, lf),
    ]
    halos = [
        go(remote(src, dst, halo_s.at[i], halo_r.at[i], row, col))
        for i, (src, dst, row, col) in enumerate(edges)
    ]

    for s in range(1, n_col):
        src = (c + n_col - s) % n_col
        mine = brow.at[src]
        remote(mine, mine, bx_s.at[s], bx_r.at[src], r, src).wait_recv()

    unit[pl.ds(0, n_col)] = brow[:, 1]
    entry = lax.broadcasted_iota(jnp.int32, (2 * n_col, n_col * 3 * STRIP), 0)
    column = lax.broadcasted_iota(jnp.int32, (2 * n_col, n_col * 3 * STRIP), 1)
    at_start = jnp.where(c == 0, 1, 0)
    at_end = jnp.where(c == n_col - 1, 1, 0)
    wanted = jnp.where(
        entry < n_col,
        (entry - at_start) * 3 * STRIP + STRIP - 1,
        (entry - n_col + at_end) * 3 * STRIP + 2 * STRIP,
    )
    pick = jnp.where(column == wanted, 1.0, 0.0).astype(BF16)
    row_all = brow[...].reshape(n_col * 3 * STRIP, brow.shape[3])
    unit[n_col] = jnp.dot(pick, row_all, preferred_element_type=F32).astype(BF16)

    d = 1 - 2 * core
    zup, zdown, yup, ydown = zrow(1), zrow(nz - 1), yrow(1), yrow(NY - 1)
    own = ball.at[r]
    go(remote(unit, own, bz_s.at[0, 0], bz_r.at[z], zup, c))
    go(remote(unit, own, bz_s.at[1, 0], bz_r.at[z], zdown, c))
    go(remote(unit, own, by_s.at[0, z], by_r.at[z, y], yup, c))
    go(remote(unit, own, by_s.at[1, z], by_r.at[z, y], ydown, c))
    ball[r] = unit[...]

    def z_arrived(step):
        src_z = (z + step + nz) % nz
        slot = ball.at[src_z * NY + y]
        remote(slot, slot, bz_s.at[0, 0], bz_r.at[src_z], r, c).wait_recv()
        return src_z, slot

    def z_forward(slot, src_z, way, to, hop):
        go(remote(slot, slot, bz_s.at[way, hop], bz_r.at[src_z], to, c))

    def y_forward(slot, src_z):
        go(remote(slot, slot, by_s.at[0, src_z], by_r.at[src_z, y], yup, c))
        go(remote(slot, slot, by_s.at[1, src_z], by_r.at[src_z, y], ydown, c))

    def y_arrived(step, src_y):
        src_z = (z + step + nz) % nz
        slot = ball.at[src_z * NY + src_y]
        remote(slot, slot, by_s.at[0, 0], by_r.at[src_z, src_y], r, c).wait_recv()
        return src_z, slot

    def y_relay(step):
        src_y = (y - d + NY) % NY
        src_z, slot = y_arrived(step, src_y)
        to = z * NY + (y + d + NY) % NY
        go(remote(slot, slot, by_s.at[2, src_z], by_r.at[src_z, src_y], to, c))

    fetches[3].wait()
    fetches[4].wait()
    fetches[5].wait()
    for i, (src, dst, row, col) in enumerate(edges):
        halos[i].wait_recv()
    zero = jnp.zeros((), F32)
    top = jnp.where(r == 0, zero, hrow[0].astype(F32))
    bottom = jnp.where(r == n_row - 1, zero, hrow[1].astype(F32))
    center = jnp.concatenate([top[None], feat_a[...].astype(F32), bottom[None]], axis=0)
    sixth = lax.broadcasted_iota(jnp.int32, (6, 1, hcol.shape[3]), 0)
    outside = ((sixth == 0) & (r == 0)) | ((sixth == 5) & (r == n_row - 1))
    left = jnp.where(outside | (c == 0), zero, hcol[0].astype(F32)[:, STRIP - 1 : STRIP])
    right = jnp.where(outside | (c == n_col - 1), zero, hcol[1].astype(F32)[:, 0:1])
    taps_a[...] = taps(center, left, right)
    n_a = 4 * feat_a.shape[1]
    total = jnp.zeros((n_a, desc_a.shape[2]), F32)
    for i in range(3):
        window = taps_a[pl.ds(i, 4)].reshape(n_a, taps_a.shape[2])
        total = total + jnp.dot(window, weight[i], preferred_element_type=F32)
    desc_a[c] = normalized(total, bias[...])
    mate = x * 2 + (1 - core)
    mine = desc_a.at[c]
    xup = ((x + 1) % nx) * 2 + core
    xdown = ((x + nx - 1) % nx) * 2 + core
    xnext = ((x + d + nx) % nx) * 2 + core
    go(remote(mine, mine, ax_s.at[0], ax_r.at[x], r, xup))
    go(remote(mine, mine, ax_s.at[1], ax_r.at[x], r, xdown))
    go(remote(mine, mine, ap_s.at[0], ap_r.at[x], r, mate))

    def x_arrived(step, hop):
        src_x = (x + step + nx) % nx
        slot = desc_a.at[src_x * 2 + core]
        remote(slot, slot, ax_s.at[0], ax_r.at[src_x], r, c).wait_recv()
        if hop == 1:
            go(remote(slot, slot, ax_s.at[2], ax_r.at[src_x], r, xnext))
        go(remote(slot, slot, ap_s.at[hop], ap_r.at[src_x], r, mate))

    for hop in (1, 2):
        for way, step, to in ((0, -hop, zup), (1, hop, zdown)):
            src_z, slot = z_arrived(step)
            z_forward(slot, src_z, way, to, hop)
            y_forward(slot, src_z)
        if hop == 1:
            y_relay(0)
        else:
            y_relay(-1)
            y_relay(1)
    z_up = (z + d + nz) % nz
    src_z, slot = z_arrived(-3 * d)
    z_forward(slot, src_z, 0, z_up * NY + y, 3)
    y_forward(slot, src_z)
    src_z, slot = z_arrived(3 * d)
    y_forward(slot, src_z)
    x_arrived(-d, 1)
    y_relay(-2)
    y_relay(2)
    x_arrived(d, 2)
    src_z, slot = z_arrived(4)
    y_forward(slot, src_z)
    y_relay(-3)
    y_relay(3)
    y_relay(4)
    x_arrived(2, 3)
    for step in (0, -1, 1, -2, 2, -3, 3, 4):
        y_arrived(step, (y + d + NY) % NY)
        y_arrived(step, (y + 2) % NY)

    listed = [lists[k, r] for k in range(KMAX)]
    live = [counts[r] > k for k in range(KMAX)]
    n_h = n_row
    n_b = n_h * STRIP
    taps_b[0] = jnp.zeros(taps_b.shape[1:], BF16)
    taps_b[n_h + 1] = jnp.zeros(taps_b.shape[1:], BF16)
    beside = ball[:, n_col].astype(F32)
    entry = lax.broadcasted_iota(jnp.int32, beside.shape, 1)
    for k in range(KMAX):
        block = ball[:, listed[k]].astype(F32)
        left = jnp.sum(jnp.where(entry == listed[k], beside, 0.0), axis=1, keepdims=True)
        right = jnp.sum(
            jnp.where(entry == listed[k] + n_col, beside, 0.0), axis=1, keepdims=True
        )
        taps_b[pl.ds(1, n_h)] = taps(block, left, right)
        total = jnp.zeros((n_b, desc_b.shape[2]), F32)
        for i in range(3):
            window = taps_b[pl.ds(i, n_h)].reshape(n_b, taps_b.shape[2])
            total = total + jnp.dot(window, weight[i], preferred_element_type=F32)
        desc_b[k] = normalized(total, bias[...])

    for s in range(nx):
        src_x = (x + s) % nx
        slot = desc_a.at[src_x * 2 + (1 - core)]
        remote(slot, slot, ap_s.at[s], ap_r.at[src_x], r, c).wait_recv()

    colacc[...] = jnp.zeros(colacc.shape, F32)
    groups = n_a // 128
    to_exp2 = scale * math.log2(math.e)

    def first(j, carry):
        cells = desc_a[j]
        rows = [jnp.zeros((1, 128), F32) for _ in range(groups)]
        for k in range(KMAX):
            found = lax.dot_general(
                desc_b[k], cells, (((1,), (1,)), ((), ())), preferred_element_type=F32
            )
            scores[k, j] = found
            acc = jnp.zeros((n_b, 128), F32)
            for g in range(groups):
                weights = jnp.exp2(found[:, g * 128 : (g + 1) * 128] * to_exp2)
                acc = acc + weights
                part = jnp.sum(weights, axis=0, keepdims=True)
                rows[g] = rows[g] + jnp.where(live[k], part, 0.0)
            colacc[k] = colacc[k] + acc
        rowpart[j] = jnp.concatenate(rows + rows, axis=0)
        return carry

    lax.fori_loop(0, n_col, first, 0)

    which = lax.broadcasted_iota(jnp.int32, (n_col, n_b), 0)
    own = jnp.zeros((n_col, n_b), F32)
    for k in range(KMAX):
        line = jnp.sum(colacc[k].T, axis=0, keepdims=True)
        own = own + jnp.where((which == listed[k]) & live[k], line, 0.0)
    for q in range(NY):
        colown[q] = own[:, q * 128 : (q + 1) * 128]
    coly[y] = colown[y]
    for s in (2, 1, 3):
        q = (y + s) % NY
        go(remote(colown.at[q], coly.at[y], cy_s.at[s], cy_r.at[y], yrow(s), c))
    for s in range(1, n_col):
        far = (c + s) % n_col
        go(remote(rowpart.at[far], rowrecv.at[c], rs_s.at[s], rs_r.at[c], r, far))
    rowrecv[c] = rowpart[c]
    for s in (1, 3, 2):
        src = (y + s) % NY
        slot = coly.at[src]
        remote(slot, slot, cy_s.at[s], cy_r.at[src], r, c).wait_recv()
    colz[z] = jnp.sum(coly[...], axis=0)
    for s in (4, 3, 5, 2, 6, 1, 7):
        go(remote(colz.at[z], colz.at[z], cz_s.at[s], cz_r.at[z], zrow(s), c))
    for s in (1, 7, 2, 6, 3, 5, 4):
        src = (z + s) % nz
        slot = colz.at[src]
        remote(slot, slot, cz_s.at[s], cz_r.at[src], r, c).wait_recv()
    logfull[y] = jnp.log(jnp.sum(colz[...], axis=0))
    for s in (2, 1, 3):
        mine = logfull.at[y]
        go(remote(mine, mine, cl_s.at[s], cl_r.at[y], yrow(s), c))
    for s in (1, 3, 2):
        src = (y + s) % NY
        slot = logfull.at[src]
        remote(slot, slot, cl_s.at[s], cl_r.at[src], r, c).wait_recv()
    logs = jnp.concatenate([logfull[q] for q in range(NY)], axis=1)
    per = 128 // STRIP
    lchunk[...] = logfull[r // per]
    lrecv[c] = lchunk[...]
    for s in range(1, n_col):
        far = (c + s) % n_col
        go(remote(lchunk, lrecv.at[c], lg_s.at[s], lg_r.at[c], r, far))

    lower = []
    for k in range(KMAX):
        line = jnp.sum(jnp.where(which == listed[k], logs, 0.0), axis=0, keepdims=True)
        lower.append(jnp.broadcast_to(line * (0.5 / scale), (128, n_b)).T)
    for k in range(KMAX):
        colacc[k] = lower[k]

    def second(j, carry):
        best = [jnp.full((1, 128), -jnp.inf, F32) for _ in range(groups)]
        for k in range(KMAX):
            for g in range(groups):
                candidate = scores[k, j, :, pl.ds(g * 128, 128)] - colacc[k]
                top_of = jnp.max(candidate, axis=0, keepdims=True)
                best[g] = jnp.maximum(best[g], jnp.where(live[k], top_of, -jnp.inf))
        maxpart[j] = jnp.concatenate(best + best, axis=0)
        return carry

    lax.fori_loop(0, n_col, second, 0)
    for s in range(1, n_col):
        far = (c + s) % n_col
        go(remote(maxpart.at[far], maxrecv.at[c], mx_s.at[s], mx_r.at[c], r, far))
    maxrecv[c] = maxpart[c]

    for s in range(1, n_col):
        src = (c + n_col - s) % n_col
        remote(rowpart.at[src], rowrecv.at[src], rs_s.at[s], rs_r.at[src], r, c).wait_recv()
        remote(lchunk, lrecv.at[src], lg_s.at[s], lg_r.at[src], r, c).wait_recv()
    row_log = jnp.log(jnp.sum(rowrecv[...], axis=0))
    lane = lax.broadcasted_iota(jnp.int32, (n_col, 128), 1)
    sub = lax.broadcasted_iota(jnp.int32, (n_col, 128), 0)
    out = jnp.zeros((n_col, 128), F32)
    for j in range(n_col):
        shift = (STRIP * j + 128 - STRIP * (r % per)) % 128
        moved = pltpu.roll(lrecv[j], shift, 1)
        out = out + jnp.where((lane // STRIP == j) & (sub == c), moved, 0.0)
    out = jnp.sum(out, axis=0, keepdims=True)
    for s in range(1, n_col):
        src = (c + n_col - s) % n_col
        remote(maxpart.at[src], maxrecv.at[src], mx_s.at[s], mx_r.at[src], r, c).wait_recv()
    best = jnp.max(maxrecv[...], axis=0) * (2.0 * scale) - row_log
    out_ref[...] = jnp.concatenate([best[0:4], jnp.broadcast_to(out, (4, 128))], axis=0)
    for copy in sends:
        copy.wait_send()


def local(feat_a, feat_b, conv_weight, conv_bias, pair_lists, pair_counts):
    n_row = lax.axis_size("row")
    n_col = lax.axis_size("col")
    ch = feat_a.shape[2]
    width = feat_a.shape[1]
    desc = conv_weight.shape[3]
    n_a = feat_a.shape[0] * width
    n_b = n_row * STRIP
    nz = n_row // NY
    nx = n_col // 2
    scale = 1.0 / (desc * 0.1)
    vmem = pl.BlockSpec(memory_space=pltpu.VMEM)
    hbm = pl.BlockSpec(memory_space=pl.ANY)
    smem = pl.BlockSpec(memory_space=pltpu.SMEM)
    dma = pltpu.SemaphoreType.DMA
    scratch = [
        pltpu.VMEM(feat_a.shape, BF16),
        pltpu.VMEM((n_col + 2, STRIP, ch), BF16),
        pltpu.VMEM((3, 3 * ch, desc), BF16),
        pltpu.VMEM((1, desc), F32),
        pltpu.VMEM((2, width, ch), BF16),
        pltpu.VMEM((2, 6, STRIP, ch), BF16),
        pltpu.VMEM((n_col, 3, STRIP, ch), BF16),
        pltpu.VMEM((n_col + 1, STRIP, ch), BF16),
        pltpu.VMEM((n_row, n_col + 1, STRIP, ch), BF16),
        pltpu.VMEM((6, width, 3 * ch), BF16),
        pltpu.VMEM((n_row + 2, STRIP, 3 * ch), BF16),
        pltpu.VMEM((n_col, n_a, desc), BF16),
        pltpu.VMEM((KMAX, n_b, desc), BF16),
        pltpu.VMEM((KMAX, n_col, n_b, n_a), F32),
        pltpu.VMEM((KMAX, n_b, 128), F32),
        pltpu.VMEM((NY, n_col, 128), F32),
        pltpu.VMEM((NY, n_col, 128), F32),
        pltpu.VMEM((nz, n_col, 128), F32),
        pltpu.VMEM((n_col, 128), F32),
        pltpu.VMEM((n_col, n_col, 128), F32),
        pltpu.VMEM((NY, n_col, 128), F32),
    ]
    scratch += [pltpu.VMEM((n_col, 8, 128), F32)] * 4
    for sent, received in (
        ((8,), (8,)),
        ((n_col,), (n_col,)),
        ((2, 4), (nz,)),
        ((3, nz), (nz, NY)),
        ((3,), (nx,)),
        ((nx,), (nx,)),
        ((NY,), (NY,)),
        ((nz,), (nz,)),
        ((n_col,), (n_col,)),
        ((n_col,), (n_col,)),
        ((n_col,), (n_col,)),
        ((NY,), (NY,)),
    ):
        scratch += [dma(sent), dma(received)]
    scratch.append(dma((6,)))
    run = pl.pallas_call(
        functools.partial(kernel, n_row, n_col, scale),
        out_shape=jax.ShapeDtypeStruct((8, 128), F32),
        in_specs=[hbm, hbm, hbm, hbm, smem, smem],
        out_specs=vmem,
        scratch_shapes=scratch,
        compiler_params=pltpu.CompilerParams(
            collective_id=0, has_side_effects=True, vmem_limit_bytes=56 * 1024 * 1024
        ),
    )
    both = run(
        feat_a,
        feat_b.reshape(width // STRIP, STRIP, ch),
        conv_weight.reshape(3, 3 * ch, desc),
        conv_bias.reshape(1, desc),
        pair_lists.T,
        pair_counts,
    )
    return (both[0:4], both[4:5])


def solution(mesh):
    in_specs = (P("row", "col", None), P("row", "col", None), P(), P(), P(), P())
    out_specs = (P("row", "col"), P("row", "col"))
    return jax.shard_map(local, mesh=mesh, in_specs=in_specs, out_specs=out_specs, check_vma=False)
```

```python
import functools
import math

import jax
import jax.numpy as jnp
from jax import lax
from jax.experimental import pallas as pl
from jax.experimental.pallas import tpu as pltpu
from jax.sharding import PartitionSpec as P

KMAX = 2
NY = 4
STRIP = 16
MESH = pl.DeviceIdType.MESH
F32 = jnp.float32
BF16 = jnp.bfloat16


def remote(src, dst, send_sem, recv_sem, row, col):
    return pltpu.make_async_remote_copy(
        src_ref=src,
        dst_ref=dst,
        send_sem=send_sem,
        recv_sem=recv_sem,
        device_id=(row, col),
        device_id_type=MESH,
    )


def taps(center, left, right):
    rows, cols, ch = center.shape
    flat = center.reshape(rows * cols, ch)
    place = lax.broadcasted_iota(jnp.int32, center.shape, 1)
    before = pltpu.roll(flat, 1, 0).reshape(center.shape)
    after = pltpu.roll(flat, rows * cols - 1, 0).reshape(center.shape)
    before = jnp.where(place == 0, left, before)
    after = jnp.where(place == cols - 1, right, after)
    return jnp.concatenate(
        [before.astype(BF16), center.astype(BF16), after.astype(BF16)], axis=2
    )


def normalized(total, bias):
    total = total + bias
    mean = jnp.mean(total * total, axis=1, keepdims=True)
    return (total * lax.rsqrt(mean + 1e-06)).astype(BF16)


def kernel(
    n_row, n_col, scale,
    feat_a_in, feat_b_in, weight_in, bias_in, lists, counts,
    out_ref,
    feat_a, tiles, weight, bias, hrow, hcol, brow, unit, ball, taps_a, taps_b, desc_a, desc_b,
    scores, colacc, coly, colz, lchunk, lrecv, logfull,
    rowpart, rowrecv, maxpart, maxrecv,
    halo_s, halo_r, bx_s, bx_r, bz_s, bz_r, by_s, by_r,
    ax_s, ax_r, ap_s, ap_r, cy_s, cy_r, cz_s, cz_r,
    rs_s, rs_r, lg_s, lg_r, mx_s, mx_r, in_sem,
):
    r = lax.axis_index("row")
    c = lax.axis_index("col")
    nz = n_row // NY
    nx = n_col // 2
    z = r // NY
    y = r % NY
    x = c // 2
    core = c % 2
    up = (r + n_row - 1) % n_row
    down = (r + 1) % n_row
    lf = (c + n_col - 1) % n_col
    rt = (c + 1) % n_col

    def zrow(step):
        return ((z + step) % nz) * NY + y

    def yrow(step):
        return z * NY + (y + step) % NY

    tail = pl.ds(n_col - 1, 1)
    fetches = [
        pltpu.make_async_copy(src, dst, in_sem.at[i])
        for i, (src, dst) in enumerate(
            [
                (feat_b_in, tiles.at[pl.ds(1, n_col)]),
                (feat_b_in.at[tail], tiles.at[pl.ds(0, 1)]),
                (feat_b_in.at[pl.ds(0, 1)], tiles.at[pl.ds(n_col + 1, 1)]),
                (feat_a_in, feat_a),
                (weight_in, weight),
                (bias_in, bias),
            ]
        )
    ]
    for fetch in fetches:
        fetch.start()
    barrier = pltpu.get_barrier_semaphore()
    partners = [(r, (c + s) % n_col) for s in range(1, n_col)]
    partners += [(yrow(1), c), (yrow(NY - 1), c), (zrow(1), c), (zrow(nz - 1), c)]
    partners += [(zrow(2), c), (zrow(nz - 2), c)]
    partners += [(v, h) for v in (up, down) for h in (lf, c, rt)]
    for device in partners:
        pl.semaphore_signal(barrier, inc=1, device_id=device, device_id_type=MESH)
    pl.semaphore_wait(barrier, len(partners))

    sends = []

    def go(copy):
        copy.start()
        sends.append(copy)
        return copy

    for fetch in fetches[:3]:
        fetch.wait()
    brow[c] = tiles[pl.ds(c, 3)]
    for s in range(1, n_col):
        far = (c + s) % n_col
        go(remote(tiles.at[pl.ds(far, 3)], brow.at[c], bx_s.at[s], bx_r.at[c], r, far))
    last = feat_a.shape[1] - STRIP
    edges = [
        (feat_a_in.at[3], hrow.at[0], down, c),
        (feat_a_in.at[0], hrow.at[1], up, c),
        (feat_a_in.at[:, pl.ds(last, STRIP)], hcol.at[0, pl.ds(1, 4)], r, rt),
        (feat_a_in.at[:, pl.ds(0, STRIP)], hcol.at[1, pl.ds(1, 4)], r, lf),
        (feat_a_in.at[3, pl.ds(last, STRIP)], hcol.at[0, 0], down, rt),
        (feat_a_in.at[3, pl.ds(0, STRIP)], hcol.at[1, 0], down, lf),
        (feat_a_in.at[0, pl.ds(last, STRIP)], hcol.at[0, 5], up, rt),
        (feat_a_in.at[0, pl.ds(0, STRIP)], hcol.at[1, 5], up, lf),
    ]
    halos = [
        go(remote(src, dst, halo_s.at[i], halo_r.at[i], row, col))
        for i, (src, dst, row, col) in enumerate(edges)
    ]

    for s in range(1, n_col):
        src = (c + n_col - s) % n_col
        mine = brow.at[src]
        remote(mine, mine, bx_s.at[s], bx_r.at[src], r, src).wait_recv()

    unit[pl.ds(0, n_col)] = brow[:, 1]
    entry = lax.broadcasted_iota(jnp.int32, (2 * n_col, n_col * 3 * STRIP), 0)
    column = lax.broadcasted_iota(jnp.int32, (2 * n_col, n_col * 3 * STRIP), 1)
    at_start = jnp.where(c == 0, 1, 0)
    at_end = jnp.where(c == n_col - 1, 1, 0)
    wanted = jnp.where(
        entry < n_col,
        (entry - at_start) * 3 * STRIP + STRIP - 1,
        (entry - n_col + at_end) * 3 * STRIP + 2 * STRIP,
    )
    pick = jnp.where(column == wanted, 1.0, 0.0).astype(BF16)
    row_all = brow[...].reshape(n_col * 3 * STRIP, brow.shape[3])
    unit[n_col] = jnp.dot(pick, row_all, preferred_element_type=F32).astype(BF16)

    d = 1 - 2 * core
    zup, zdown, yup, ydown = zrow(1), zrow(nz - 1), yrow(1), yrow(NY - 1)
    own = ball.at[r]
    go(remote(unit, own, bz_s.at[0, 0], bz_r.at[z], zup, c))
    go(remote(unit, own, bz_s.at[1, 0], bz_r.at[z], zdown, c))
    go(remote(unit, own, bz_s.at[0, 1], bz_r.at[z], zrow(2), c))
    go(remote(unit, own, bz_s.at[1, 1], bz_r.at[z], zrow(nz - 2), c))
    go(remote(unit, own, by_s.at[0, z], by_r.at[z, y], yup, c))
    go(remote(unit, own, by_s.at[1, z], by_r.at[z, y], ydown, c))
    ball[r] = unit[...]

    def z_arrived(step):
        src_z = (z + step + nz) % nz
        slot = ball.at[src_z * NY + y]
        remote(slot, slot, bz_s.at[0, 0], bz_r.at[src_z], r, c).wait_recv()
        return src_z, slot

    def z_forward(slot, src_z, way, to, hop):
        go(remote(slot, slot, bz_s.at[way, hop], bz_r.at[src_z], to, c))

    def y_forward(slot, src_z):
        go(remote(slot, slot, by_s.at[0, src_z], by_r.at[src_z, y], yup, c))
        go(remote(slot, slot, by_s.at[1, src_z], by_r.at[src_z, y], ydown, c))

    def y_arrived(step, src_y):
        src_z = (z + step + nz) % nz
        slot = ball.at[src_z * NY + src_y]
        remote(slot, slot, by_s.at[0, 0], by_r.at[src_z, src_y], r, c).wait_recv()
        return src_z, slot

    def y_relay(step):
        src_y = (y - d + NY) % NY
        src_z, slot = y_arrived(step, src_y)
        to = z * NY + (y + d + NY) % NY
        go(remote(slot, slot, by_s.at[2, src_z], by_r.at[src_z, src_y], to, c))

    mate = x * 2 + (1 - core)
    fetches[3].wait()
    fetches[4].wait()
    fetches[5].wait()
    for i, (src, dst, row, col) in enumerate(edges):
        halos[i].wait_recv()
    zero = jnp.zeros((), F32)
    top = jnp.where(r == 0, zero, hrow[0].astype(F32))
    bottom = jnp.where(r == n_row - 1, zero, hrow[1].astype(F32))
    center = jnp.concatenate([top[None], feat_a[...].astype(F32), bottom[None]], axis=0)
    sixth = lax.broadcasted_iota(jnp.int32, (6, 1, hcol.shape[3]), 0)
    outside = ((sixth == 0) & (r == 0)) | ((sixth == 5) & (r == n_row - 1))
    left = jnp.where(outside | (c == 0), zero, hcol[0].astype(F32)[:, STRIP - 1 : STRIP])
    right = jnp.where(outside | (c == n_col - 1), zero, hcol[1].astype(F32)[:, 0:1])
    taps_a[...] = taps(center, left, right)
    n_a = 4 * feat_a.shape[1]
    total = jnp.zeros((n_a, desc_a.shape[2]), F32)
    for i in range(3):
        window = taps_a[pl.ds(i, 4)].reshape(n_a, taps_a.shape[2])
        total = total + jnp.dot(window, weight[i], preferred_element_type=F32)
    desc_a[c] = normalized(total, bias[...])
    mine = desc_a.at[c]
    xup = ((x + 1) % nx) * 2 + core
    xdown = ((x + nx - 1) % nx) * 2 + core
    xnext = ((x + d + nx) % nx) * 2 + core
    go(remote(mine, mine, ax_s.at[0], ax_r.at[x], r, xup))
    go(remote(mine, mine, ax_s.at[1], ax_r.at[x], r, xdown))
    go(remote(mine, mine, ap_s.at[0], ap_r.at[x], r, mate))

    def x_arrived(step, hop):
        src_x = (x + step + nx) % nx
        slot = desc_a.at[src_x * 2 + core]
        remote(slot, slot, ax_s.at[0], ax_r.at[src_x], r, c).wait_recv()
        if hop == 1:
            go(remote(slot, slot, ax_s.at[2], ax_r.at[src_x], r, xnext))
        go(remote(slot, slot, ap_s.at[hop], ap_r.at[src_x], r, mate))

    for step in (-1, 1):
        src_z, slot = z_arrived(step)
        y_forward(slot, src_z)
    y_relay(0)
    z_far = ((z + 2 * d + nz) % nz) * NY + y
    src_z, slot = z_arrived(-2 * d)
    z_forward(slot, src_z, 0, z_far, 3)
    z_forward(slot, src_z, 0, ((z + d + nz) % nz) * NY + y, 2)
    y_forward(slot, src_z)
    src_z, slot = z_arrived(2 * d)
    z_forward(slot, src_z, 1, ((z - d + nz) % nz) * NY + y, 2)
    y_forward(slot, src_z)
    y_relay(-1)
    y_relay(1)
    for step in (-3, 3):
        src_z, slot = z_arrived(step)
        y_forward(slot, src_z)
    x_arrived(-d, 1)
    y_relay(-2)
    y_relay(2)
    x_arrived(d, 2)
    src_z, slot = z_arrived(4)
    y_forward(slot, src_z)
    y_relay(-3)
    y_relay(3)
    y_relay(4)
    x_arrived(2, 3)
    for step in (0, -1, 1, -2, 2, -3, 3, 4):
        y_arrived(step, (y + d + NY) % NY)
        y_arrived(step, (y + 2) % NY)

    listed = [lists[k, r] for k in range(KMAX)]
    live = [counts[r] > k for k in range(KMAX)]
    n_h = n_row
    n_b = n_h * STRIP
    taps_b[0] = jnp.zeros(taps_b.shape[1:], BF16)
    taps_b[n_h + 1] = jnp.zeros(taps_b.shape[1:], BF16)
    beside = ball[:, n_col].astype(F32)
    entry = lax.broadcasted_iota(jnp.int32, beside.shape, 1)
    for k in range(KMAX):
        block = ball[:, listed[k]].astype(F32)
        left = jnp.sum(jnp.where(entry == listed[k], beside, 0.0), axis=1, keepdims=True)
        right = jnp.sum(
            jnp.where(entry == listed[k] + n_col, beside, 0.0), axis=1, keepdims=True
        )
        taps_b[pl.ds(1, n_h)] = taps(block, left, right)
        total = jnp.zeros((n_b, desc_b.shape[2]), F32)
        for i in range(3):
            window = taps_b[pl.ds(i, n_h)].reshape(n_b, taps_b.shape[2])
            total = total + jnp.dot(window, weight[i], preferred_element_type=F32)
        desc_b[k] = normalized(total, bias[...])

    for s in range(nx):
        src_x = (x + s) % nx
        slot = desc_a.at[src_x * 2 + (1 - core)]
        remote(slot, slot, ap_s.at[s], ap_r.at[src_x], r, c).wait_recv()

    colacc[...] = jnp.zeros(colacc.shape, F32)
    groups = n_a // 128
    to_exp2 = scale * math.log2(math.e)

    def first(j, carry):
        cells = desc_a[j]
        rows = [jnp.zeros((1, 128), F32) for _ in range(groups)]
        for k in range(KMAX):
            found = lax.dot_general(
                desc_b[k], cells, (((1,), (1,)), ((), ())), preferred_element_type=F32
            )
            scores[k, j] = found
            acc = jnp.zeros((n_b, 128), F32)
            for g in range(groups):
                weights = jnp.exp2(found[:, g * 128 : (g + 1) * 128] * to_exp2)
                acc = acc + weights
                part = jnp.sum(weights, axis=0, keepdims=True)
                rows[g] = rows[g] + jnp.where(live[k], part, 0.0)
            colacc[k] = colacc[k] + acc
        rowpart[j] = jnp.concatenate(rows + rows, axis=0)
        return carry

    lax.fori_loop(0, n_col, first, 0)

    which = lax.broadcasted_iota(jnp.int32, (n_col, n_b), 0)
    own = jnp.zeros((n_col, n_b), F32)
    for k in range(KMAX):
        line = jnp.sum(colacc[k].T, axis=0, keepdims=True)
        own = own + jnp.where((which == listed[k]) & live[k], line, 0.0)
    coly[y] = own
    for s in (2, 1, 3):
        go(remote(coly.at[y], coly.at[y], cy_s.at[s], cy_r.at[y], yrow(s), c))
    for s in range(1, n_col):
        far = (c + s) % n_col
        go(remote(rowpart.at[far], rowrecv.at[c], rs_s.at[s], rs_r.at[c], r, far))
    rowrecv[c] = rowpart[c]
    for s in (1, 3, 2):
        src = (y + s) % NY
        slot = coly.at[src]
        remote(slot, slot, cy_s.at[s], cy_r.at[src], r, c).wait_recv()
    colz[z] = jnp.sum(coly[...], axis=0)
    for s in (4, 3, 5, 2, 6, 1, 7):
        go(remote(colz.at[z], colz.at[z], cz_s.at[s], cz_r.at[z], zrow(s), c))
    for s in (1, 7, 2, 6, 3, 5, 4):
        src = (z + s) % nz
        slot = colz.at[src]
        remote(slot, slot, cz_s.at[s], cz_r.at[src], r, c).wait_recv()
    logs = jnp.log(jnp.sum(colz[...], axis=0))
    for q in range(NY):
        logfull[q] = logs[:, q * 128 : (q + 1) * 128]
    per = 128 // STRIP
    lchunk[...] = logfull[r // per]
    lrecv[c] = lchunk[...]
    for s in range(1, n_col):
        far = (c + s) % n_col
        go(remote(lchunk, lrecv.at[c], lg_s.at[s], lg_r.at[c], r, far))

    lower = []
    for k in range(KMAX):
        line = jnp.sum(jnp.where(which == listed[k], logs, 0.0), axis=0, keepdims=True)
        lower.append(jnp.broadcast_to(line * (0.5 / scale), (128, n_b)).T)
    for k in range(KMAX):
        colacc[k] = lower[k]

    def second(j, carry):
        best = [jnp.full((1, 128), -jnp.inf, F32) for _ in range(groups)]
        for k in range(KMAX):
            for g in range(groups):
                candidate = scores[k, j, :, pl.ds(g * 128, 128)] - colacc[k]
                top_of = jnp.max(candidate, axis=0, keepdims=True)
                best[g] = jnp.maximum(best[g], jnp.where(live[k], top_of, -jnp.inf))
        maxpart[j] = jnp.concatenate(best + best, axis=0)
        return carry

    lax.fori_loop(0, n_col, second, 0)
    for s in range(1, n_col):
        far = (c + s) % n_col
        go(remote(maxpart.at[far], maxrecv.at[c], mx_s.at[s], mx_r.at[c], r, far))
    maxrecv[c] = maxpart[c]

    for s in range(1, n_col):
        src = (c + n_col - s) % n_col
        remote(rowpart.at[src], rowrecv.at[src], rs_s.at[s], rs_r.at[src], r, c).wait_recv()
        remote(lchunk, lrecv.at[src], lg_s.at[s], lg_r.at[src], r, c).wait_recv()
    row_log = jnp.log(jnp.sum(rowrecv[...], axis=0))
    lane = lax.broadcasted_iota(jnp.int32, (n_col, 128), 1)
    sub = lax.broadcasted_iota(jnp.int32, (n_col, 128), 0)
    out = jnp.zeros((n_col, 128), F32)
    for j in range(n_col):
        shift = (STRIP * j + 128 - STRIP * (r % per)) % 128
        moved = pltpu.roll(lrecv[j], shift, 1)
        out = out + jnp.where((lane // STRIP == j) & (sub == c), moved, 0.0)
    out = jnp.sum(out, axis=0, keepdims=True)
    for s in range(1, n_col):
        src = (c + n_col - s) % n_col
        remote(maxpart.at[src], maxrecv.at[src], mx_s.at[s], mx_r.at[src], r, c).wait_recv()
    best = jnp.max(maxrecv[...], axis=0) * (2.0 * scale) - row_log
    out_ref[...] = jnp.concatenate([best[0:4], jnp.broadcast_to(out, (4, 128))], axis=0)
    for copy in sends:
        copy.wait_send()


def local(feat_a, feat_b, conv_weight, conv_bias, pair_lists, pair_counts):
    n_row = lax.axis_size("row")
    n_col = lax.axis_size("col")
    ch = feat_a.shape[2]
    width = feat_a.shape[1]
    desc = conv_weight.shape[3]
    n_a = feat_a.shape[0] * width
    n_b = n_row * STRIP
    nz = n_row // NY
    nx = n_col // 2
    scale = 1.0 / (desc * 0.1)
    vmem = pl.BlockSpec(memory_space=pltpu.VMEM)
    hbm = pl.BlockSpec(memory_space=pl.ANY)
    smem = pl.BlockSpec(memory_space=pltpu.SMEM)
    dma = pltpu.SemaphoreType.DMA
    scratch = [
        pltpu.VMEM(feat_a.shape, BF16),
        pltpu.VMEM((n_col + 2, STRIP, ch), BF16),
        pltpu.VMEM((3, 3 * ch, desc), BF16),
        pltpu.VMEM((1, desc), F32),
        pltpu.VMEM((2, width, ch), BF16),
        pltpu.VMEM((2, 6, STRIP, ch), BF16),
        pltpu.VMEM((n_col, 3, STRIP, ch), BF16),
        pltpu.VMEM((n_col + 1, STRIP, ch), BF16),
        pltpu.VMEM((n_row, n_col + 1, STRIP, ch), BF16),
        pltpu.VMEM((6, width, 3 * ch), BF16),
        pltpu.VMEM((n_row + 2, STRIP, 3 * ch), BF16),
        pltpu.VMEM((n_col, n_a, desc), BF16),
        pltpu.VMEM((KMAX, n_b, desc), BF16),
        pltpu.VMEM((KMAX, n_col, n_b, n_a), F32),
        pltpu.VMEM((KMAX, n_b, 128), F32),
        pltpu.VMEM((NY, n_col, n_b), F32),
        pltpu.VMEM((nz, n_col, n_b), F32),
        pltpu.VMEM((n_col, 128), F32),
        pltpu.VMEM((n_col, n_col, 128), F32),
        pltpu.VMEM((NY, n_col, 128), F32),
    ]
    scratch += [pltpu.VMEM((n_col, 8, 128), F32)] * 4
    for sent, received in (
        ((8,), (8,)),
        ((n_col,), (n_col,)),
        ((2, 4), (nz,)),
        ((3, nz), (nz, NY)),
        ((3,), (nx,)),
        ((nx,), (nx,)),
        ((NY,), (NY,)),
        ((nz,), (nz,)),
        ((n_col,), (n_col,)),
        ((n_col,), (n_col,)),
        ((n_col,), (n_col,)),
    ):
        scratch += [dma(sent), dma(received)]
    scratch.append(dma((6,)))
    run = pl.pallas_call(
        functools.partial(kernel, n_row, n_col, scale),
        out_shape=jax.ShapeDtypeStruct((8, 128), F32),
        in_specs=[hbm, hbm, hbm, hbm, smem, smem],
        out_specs=vmem,
        scratch_shapes=scratch,
        compiler_params=pltpu.CompilerParams(
            collective_id=0, has_side_effects=True, vmem_limit_bytes=56 * 1024 * 1024
        ),
    )
    both = run(
        feat_a,
        feat_b.reshape(width // STRIP, STRIP, ch),
        conv_weight.reshape(3, 3 * ch, desc),
        conv_bias.reshape(1, desc),
        pair_lists.T,
        pair_counts,
    )
    return (both[0:4], both[4:5])


def solution(mesh):
    in_specs = (P("row", "col", None), P("row", "col", None), P(), P(), P(), P())
    out_specs = (P("row", "col"), P("row", "col"))
    return jax.shard_map(local, mesh=mesh, in_specs=in_specs, out_specs=out_specs, check_vma=False)
```

```python
import functools
import math

import jax
import jax.numpy as jnp
from jax import lax
from jax.experimental import pallas as pl
from jax.experimental.pallas import tpu as pltpu
from jax.sharding import PartitionSpec as P

KMAX = 2
NY = 4
STRIP = 16
MESH = pl.DeviceIdType.MESH
F32 = jnp.float32
BF16 = jnp.bfloat16


def remote(src, dst, send_sem, recv_sem, row, col):
    return pltpu.make_async_remote_copy(
        src_ref=src,
        dst_ref=dst,
        send_sem=send_sem,
        recv_sem=recv_sem,
        device_id=(row, col),
        device_id_type=MESH,
    )


def taps(center, left, right):
    rows, cols, ch = center.shape
    flat = center.reshape(rows * cols, ch)
    place = lax.broadcasted_iota(jnp.int32, center.shape, 1)
    before = pltpu.roll(flat, 1, 0).reshape(center.shape)
    after = pltpu.roll(flat, rows * cols - 1, 0).reshape(center.shape)
    before = jnp.where(place == 0, left, before)
    after = jnp.where(place == cols - 1, right, after)
    return jnp.concatenate(
        [before.astype(BF16), center.astype(BF16), after.astype(BF16)], axis=2
    )


def normalized(total, bias):
    total = total + bias
    mean = jnp.mean(total * total, axis=1, keepdims=True)
    return (total * lax.rsqrt(mean + 1e-06)).astype(BF16)


def kernel(
    n_row, n_col, scale,
    feat_a_in, feat_b_in, weight_in, bias_in, lists, counts,
    out_ref,
    feat_a, tiles, weight, bias, hrow, hcol, brow, unit, ball, taps_a, taps_b, desc_a, desc_b,
    scores, colacc, coly, colz, lchunk, lrecv, logfull,
    rowpart, rowrecv, maxpart, maxrecv,
    halo_s, halo_r, bx_s, bx_r, bz_s, bz_r, by_s, by_r,
    ax_s, ax_r, ap_s, ap_r, cy_s, cy_r, cz_s, cz_r,
    rs_s, rs_r, lg_s, lg_r, mx_s, mx_r, in_sem,
):
    r = lax.axis_index("row")
    c = lax.axis_index("col")
    nz = n_row // NY
    nx = n_col // 2
    z = r // NY
    y = r % NY
    x = c // 2
    core = c % 2
    up = (r + n_row - 1) % n_row
    down = (r + 1) % n_row
    lf = (c + n_col - 1) % n_col
    rt = (c + 1) % n_col

    def zrow(step):
        return ((z + step) % nz) * NY + y

    def yrow(step):
        return z * NY + (y + step) % NY

    tail = pl.ds(n_col - 1, 1)
    fetches = [
        pltpu.make_async_copy(src, dst, in_sem.at[i])
        for i, (src, dst) in enumerate(
            [
                (feat_b_in, tiles.at[pl.ds(1, n_col)]),
                (feat_b_in.at[tail], tiles.at[pl.ds(0, 1)]),
                (feat_b_in.at[pl.ds(0, 1)], tiles.at[pl.ds(n_col + 1, 1)]),
                (feat_a_in, feat_a),
                (weight_in, weight),
                (bias_in, bias),
            ]
        )
    ]
    for fetch in fetches:
        fetch.start()
    barrier = pltpu.get_barrier_semaphore()
    partners = [(r, (c + s) % n_col) for s in range(1, n_col)]
    partners += [(yrow(1), c), (yrow(NY - 1), c), (zrow(1), c), (zrow(nz - 1), c)]
    partners += [(zrow(2), c), (zrow(nz - 2), c)]
    partners += [(v, h) for v in (up, down) for h in (lf, c, rt)]
    for device in partners:
        pl.semaphore_signal(barrier, inc=1, device_id=device, device_id_type=MESH)
    pl.semaphore_wait(barrier, len(partners))

    sends = []

    def go(copy):
        copy.start()
        sends.append(copy)
        return copy

    for fetch in fetches[:3]:
        fetch.wait()
    brow[c] = tiles[pl.ds(c, 3)]
    for s in range(1, n_col):
        far = (c + s) % n_col
        go(remote(tiles.at[pl.ds(far, 3)], brow.at[c], bx_s.at[s], bx_r.at[c], r, far))
    last = feat_a.shape[1] - STRIP
    edges = [
        (feat_a_in.at[3], hrow.at[0], down, c),
        (feat_a_in.at[0], hrow.at[1], up, c),
        (feat_a_in.at[:, pl.ds(last, STRIP)], hcol.at[0, pl.ds(1, 4)], r, rt),
        (feat_a_in.at[:, pl.ds(0, STRIP)], hcol.at[1, pl.ds(1, 4)], r, lf),
        (feat_a_in.at[3, pl.ds(last, STRIP)], hcol.at[0, 0], down, rt),
        (feat_a_in.at[3, pl.ds(0, STRIP)], hcol.at[1, 0], down, lf),
        (feat_a_in.at[0, pl.ds(last, STRIP)], hcol.at[0, 5], up, rt),
        (feat_a_in.at[0, pl.ds(0, STRIP)], hcol.at[1, 5], up, lf),
    ]
    halos = [
        go(remote(src, dst, halo_s.at[i], halo_r.at[i], row, col))
        for i, (src, dst, row, col) in enumerate(edges)
    ]

    for s in range(1, n_col):
        src = (c + n_col - s) % n_col
        mine = brow.at[src]
        remote(mine, mine, bx_s.at[s], bx_r.at[src], r, src).wait_recv()

    unit[pl.ds(0, n_col)] = brow[:, 1]
    entry = lax.broadcasted_iota(jnp.int32, (2 * n_col, n_col * 3 * STRIP), 0)
    column = lax.broadcasted_iota(jnp.int32, (2 * n_col, n_col * 3 * STRIP), 1)
    at_start = jnp.where(c == 0, 1, 0)
    at_end = jnp.where(c == n_col - 1, 1, 0)
    wanted = jnp.where(
        entry < n_col,
        (entry - at_start) * 3 * STRIP + STRIP - 1,
        (entry - n_col + at_end) * 3 * STRIP + 2 * STRIP,
    )
    pick = jnp.where(column == wanted, 1.0, 0.0).astype(BF16)
    row_all = brow[...].reshape(n_col * 3 * STRIP, brow.shape[3])
    unit[n_col] = jnp.dot(pick, row_all, preferred_element_type=F32).astype(BF16)

    d = 1 - 2 * core
    zup, zdown, yup, ydown = zrow(1), zrow(nz - 1), yrow(1), yrow(NY - 1)
    own = ball.at[r]
    go(remote(unit, own, bz_s.at[0, 0], bz_r.at[z], zup, c))
    go(remote(unit, own, bz_s.at[1, 0], bz_r.at[z], zdown, c))
    go(remote(unit, own, bz_s.at[0, 1], bz_r.at[z], zrow(2), c))
    go(remote(unit, own, bz_s.at[1, 1], bz_r.at[z], zrow(nz - 2), c))
    go(remote(unit, own, by_s.at[0, z], by_r.at[z, y], yup, c))
    go(remote(unit, own, by_s.at[1, z], by_r.at[z, y], ydown, c))
    ball[r] = unit[...]

    def z_arrived(step):
        src_z = (z + step + nz) % nz
        slot = ball.at[src_z * NY + y]
        remote(slot, slot, bz_s.at[0, 0], bz_r.at[src_z], r, c).wait_recv()
        return src_z, slot

    def z_forward(slot, src_z, way, to, hop):
        go(remote(slot, slot, bz_s.at[way, hop], bz_r.at[src_z], to, c))

    def y_forward(slot, src_z):
        go(remote(slot, slot, by_s.at[0, src_z], by_r.at[src_z, y], yup, c))
        go(remote(slot, slot, by_s.at[1, src_z], by_r.at[src_z, y], ydown, c))

    def y_arrived(step, src_y):
        src_z = (z + step + nz) % nz
        slot = ball.at[src_z * NY + src_y]
        remote(slot, slot, by_s.at[0, 0], by_r.at[src_z, src_y], r, c).wait_recv()
        return src_z, slot

    def y_relay(step):
        src_y = (y - d + NY) % NY
        src_z, slot = y_arrived(step, src_y)
        to = z * NY + (y + d + NY) % NY
        go(remote(slot, slot, by_s.at[2, src_z], by_r.at[src_z, src_y], to, c))

    mate = x * 2 + (1 - core)
    fetches[3].wait()
    fetches[4].wait()
    fetches[5].wait()
    for i, (src, dst, row, col) in enumerate(edges):
        halos[i].wait_recv()
    zero = jnp.zeros((), F32)
    top = jnp.where(r == 0, zero, hrow[0].astype(F32))
    bottom = jnp.where(r == n_row - 1, zero, hrow[1].astype(F32))
    center = jnp.concatenate([top[None], feat_a[...].astype(F32), bottom[None]], axis=0)
    sixth = lax.broadcasted_iota(jnp.int32, (6, 1, hcol.shape[3]), 0)
    outside = ((sixth == 0) & (r == 0)) | ((sixth == 5) & (r == n_row - 1))
    left = jnp.where(outside | (c == 0), zero, hcol[0].astype(F32)[:, STRIP - 1 : STRIP])
    right = jnp.where(outside | (c == n_col - 1), zero, hcol[1].astype(F32)[:, 0:1])
    taps_a[...] = taps(center, left, right)
    n_a = 4 * feat_a.shape[1]
    total = jnp.zeros((n_a, desc_a.shape[2]), F32)
    for i in range(3):
        window = taps_a[pl.ds(i, 4)].reshape(n_a, taps_a.shape[2])
        total = total + jnp.dot(window, weight[i], preferred_element_type=F32)
    desc_a[c] = normalized(total, bias[...])
    mine = desc_a.at[c]
    xup = ((x + 1) % nx) * 2 + core
    xdown = ((x + nx - 1) % nx) * 2 + core
    xnext = ((x + d + nx) % nx) * 2 + core
    go(remote(mine, mine, ax_s.at[0], ax_r.at[x], r, xup))
    go(remote(mine, mine, ax_s.at[1], ax_r.at[x], r, xdown))
    go(remote(mine, mine, ap_s.at[0], ap_r.at[x], r, mate))

    def x_arrived(step, hop):
        src_x = (x + step + nx) % nx
        slot = desc_a.at[src_x * 2 + core]
        remote(slot, slot, ax_s.at[0], ax_r.at[src_x], r, c).wait_recv()
        if hop == 1:
            go(remote(slot, slot, ax_s.at[2], ax_r.at[src_x], r, xnext))
        go(remote(slot, slot, ap_s.at[hop], ap_r.at[src_x], r, mate))

    for step in (-1, 1):
        src_z, slot = z_arrived(step)
        y_forward(slot, src_z)
    y_relay(0)
    z_far = ((z + 2 * d + nz) % nz) * NY + y
    src_z, slot = z_arrived(-2 * d)
    z_forward(slot, src_z, 0, z_far, 3)
    z_forward(slot, src_z, 0, ((z + d + nz) % nz) * NY + y, 2)
    y_forward(slot, src_z)
    src_z, slot = z_arrived(2 * d)
    z_forward(slot, src_z, 1, ((z - d + nz) % nz) * NY + y, 2)
    y_forward(slot, src_z)
    y_relay(-1)
    y_relay(1)
    for step in (-3, 3):
        src_z, slot = z_arrived(step)
        y_forward(slot, src_z)
    x_arrived(-d, 1)
    y_relay(-2)
    y_relay(2)
    x_arrived(d, 2)
    src_z, slot = z_arrived(4)
    y_forward(slot, src_z)
    y_relay(-3)
    y_relay(3)
    y_relay(4)
    x_arrived(2, 3)
    for step in (0, -1, 1, -2, 2, -3, 3, 4):
        y_arrived(step, (y + d + NY) % NY)
        y_arrived(step, (y + 2) % NY)

    listed = [lists[k, r] for k in range(KMAX)]
    live = [counts[r] > k for k in range(KMAX)]
    n_h = n_row
    n_b = n_h * STRIP
    taps_b[0] = jnp.zeros(taps_b.shape[1:], BF16)
    taps_b[n_h + 1] = jnp.zeros(taps_b.shape[1:], BF16)
    beside = ball[:, n_col].astype(F32)
    entry = lax.broadcasted_iota(jnp.int32, beside.shape, 1)
    for k in range(KMAX):
        block = ball[:, listed[k]].astype(F32)
        left = jnp.sum(jnp.where(entry == listed[k], beside, 0.0), axis=1, keepdims=True)
        right = jnp.sum(
            jnp.where(entry == listed[k] + n_col, beside, 0.0), axis=1, keepdims=True
        )
        taps_b[pl.ds(1, n_h)] = taps(block, left, right)
        total = jnp.zeros((n_b, desc_b.shape[2]), F32)
        for i in range(3):
            window = taps_b[pl.ds(i, n_h)].reshape(n_b, taps_b.shape[2])
            total = total + jnp.dot(window, weight[i], preferred_element_type=F32)
        desc_b[k] = normalized(total, bias[...])

    for s in range(nx):
        src_x = (x + s) % nx
        slot = desc_a.at[src_x * 2 + (1 - core)]
        remote(slot, slot, ap_s.at[s], ap_r.at[src_x], r, c).wait_recv()

    colacc[...] = jnp.zeros(colacc.shape, F32)
    groups = n_a // 128
    to_exp2 = scale * math.log2(math.e)

    def first(j, carry):
        cells = desc_a[j]
        rows = [jnp.zeros((1, 128), F32) for _ in range(groups)]
        for k in range(KMAX):
            found = lax.dot_general(
                desc_b[k], cells, (((1,), (1,)), ((), ())), preferred_element_type=F32
            )
            scores[k, j] = found
            acc = jnp.zeros((n_b, 128), F32)
            for g in range(groups):
                weights = jnp.exp2(found[:, g * 128 : (g + 1) * 128] * to_exp2)
                acc = acc + weights
                part = jnp.sum(weights, axis=0, keepdims=True)
                rows[g] = rows[g] + jnp.where(live[k], part, 0.0)
            colacc[k] = colacc[k] + acc
        rowpart[j] = jnp.concatenate(rows + rows, axis=0)
        return carry

    lax.fori_loop(0, n_col, first, 0, unroll=2)

    which = lax.broadcasted_iota(jnp.int32, (n_col, n_b), 0)
    own = jnp.zeros((n_col, n_b), F32)
    for k in range(KMAX):
        line = jnp.sum(colacc[k].T, axis=0, keepdims=True)
        own = own + jnp.where((which == listed[k]) & live[k], line, 0.0)
    coly[y] = own
    for s in (2, 1, 3):
        go(remote(coly.at[y], coly.at[y], cy_s.at[s], cy_r.at[y], yrow(s), c))
    for s in range(1, n_col):
        far = (c + s) % n_col
        go(remote(rowpart.at[far], rowrecv.at[c], rs_s.at[s], rs_r.at[c], r, far))
    rowrecv[c] = rowpart[c]
    for s in (1, 3, 2):
        src = (y + s) % NY
        slot = coly.at[src]
        remote(slot, slot, cy_s.at[s], cy_r.at[src], r, c).wait_recv()
    colz[z] = jnp.sum(coly[...], axis=0)
    for s in (4, 3, 5, 2, 6, 1, 7):
        go(remote(colz.at[z], colz.at[z], cz_s.at[s], cz_r.at[z], zrow(s), c))
    for s in (1, 7, 2, 6, 3, 5, 4):
        src = (z + s) % nz
        slot = colz.at[src]
        remote(slot, slot, cz_s.at[s], cz_r.at[src], r, c).wait_recv()
    logs = jnp.log(jnp.sum(colz[...], axis=0))
    for q in range(NY):
        logfull[q] = logs[:, q * 128 : (q + 1) * 128]
    per = 128 // STRIP
    lchunk[...] = logfull[r // per]
    lrecv[c] = lchunk[...]
    for s in range(1, n_col):
        far = (c + s) % n_col
        go(remote(lchunk, lrecv.at[c], lg_s.at[s], lg_r.at[c], r, far))

    lower = []
    for k in range(KMAX):
        line = jnp.sum(jnp.where(which == listed[k], logs, 0.0), axis=0, keepdims=True)
        lower.append(jnp.broadcast_to(line * (0.5 / scale), (128, n_b)).T)
    for k in range(KMAX):
        colacc[k] = lower[k]

    def second(turn, carry):
        j = (c + 1 + turn) % n_col
        best = [jnp.full((1, 128), -jnp.inf, F32) for _ in range(groups)]
        for k in range(KMAX):
            for g in range(groups):
                candidate = scores[k, j, :, pl.ds(g * 128, 128)] - colacc[k]
                top_of = jnp.max(candidate, axis=0, keepdims=True)
                best[g] = jnp.maximum(best[g], jnp.where(live[k], top_of, -jnp.inf))
        maxpart[j] = jnp.concatenate(best + best, axis=0)

        @pl.when(turn < n_col - 1)
        def _():
            slot = turn + 1
            remote(maxpart.at[j], maxrecv.at[c], mx_s.at[slot], mx_r.at[c], r, j).start()

        return carry

    lax.fori_loop(0, n_col, second, 0, unroll=2)
    for s in range(1, n_col):
        far = (c + s) % n_col
        sends.append(remote(maxpart.at[far], maxrecv.at[c], mx_s.at[s], mx_r.at[c], r, far))
    maxrecv[c] = maxpart[c]

    for s in range(1, n_col):
        src = (c + n_col - s) % n_col
        remote(rowpart.at[src], rowrecv.at[src], rs_s.at[s], rs_r.at[src], r, c).wait_recv()
        remote(lchunk, lrecv.at[src], lg_s.at[s], lg_r.at[src], r, c).wait_recv()
    row_log = jnp.log(jnp.sum(rowrecv[...], axis=0))
    lane = lax.broadcasted_iota(jnp.int32, (n_col, 128), 1)
    sub = lax.broadcasted_iota(jnp.int32, (n_col, 128), 0)
    out = jnp.zeros((n_col, 128), F32)
    for j in range(n_col):
        shift = (STRIP * j + 128 - STRIP * (r % per)) % 128
        moved = pltpu.roll(lrecv[j], shift, 1)
        out = out + jnp.where((lane // STRIP == j) & (sub == c), moved, 0.0)
    out = jnp.sum(out, axis=0, keepdims=True)
    for s in range(1, n_col):
        src = (c + n_col - s) % n_col
        remote(maxpart.at[src], maxrecv.at[src], mx_s.at[s], mx_r.at[src], r, c).wait_recv()
    best = jnp.max(maxrecv[...], axis=0) * (2.0 * scale) - row_log
    out_ref[...] = jnp.concatenate([best[0:4], jnp.broadcast_to(out, (4, 128))], axis=0)
    for copy in sends:
        copy.wait_send()


def local(feat_a, feat_b, conv_weight, conv_bias, pair_lists, pair_counts):
    n_row = lax.axis_size("row")
    n_col = lax.axis_size("col")
    ch = feat_a.shape[2]
    width = feat_a.shape[1]
    desc = conv_weight.shape[3]
    n_a = feat_a.shape[0] * width
    n_b = n_row * STRIP
    nz = n_row // NY
    nx = n_col // 2
    scale = 1.0 / (desc * 0.1)
    vmem = pl.BlockSpec(memory_space=pltpu.VMEM)
    hbm = pl.BlockSpec(memory_space=pl.ANY)
    smem = pl.BlockSpec(memory_space=pltpu.SMEM)
    dma = pltpu.SemaphoreType.DMA
    scratch = [
        pltpu.VMEM(feat_a.shape, BF16),
        pltpu.VMEM((n_col + 2, STRIP, ch), BF16),
        pltpu.VMEM((3, 3 * ch, desc), BF16),
        pltpu.VMEM((1, desc), F32),
        pltpu.VMEM((2, width, ch), BF16),
        pltpu.VMEM((2, 6, STRIP, ch), BF16),
        pltpu.VMEM((n_col, 3, STRIP, ch), BF16),
        pltpu.VMEM((n_col + 1, STRIP, ch), BF16),
        pltpu.VMEM((n_row, n_col + 1, STRIP, ch), BF16),
        pltpu.VMEM((6, width, 3 * ch), BF16),
        pltpu.VMEM((n_row + 2, STRIP, 3 * ch), BF16),
        pltpu.VMEM((n_col, n_a, desc), BF16),
        pltpu.VMEM((KMAX, n_b, desc), BF16),
        pltpu.VMEM((KMAX, n_col, n_b, n_a), F32),
        pltpu.VMEM((KMAX, n_b, 128), F32),
        pltpu.VMEM((NY, n_col, n_b), F32),
        pltpu.VMEM((nz, n_col, n_b), F32),
        pltpu.VMEM((n_col, 128), F32),
        pltpu.VMEM((n_col, n_col, 128), F32),
        pltpu.VMEM((NY, n_col, 128), F32),
    ]
    scratch += [pltpu.VMEM((n_col, 8, 128), F32)] * 4
    for sent, received in (
        ((8,), (8,)),
        ((n_col,), (n_col,)),
        ((2, 4), (nz,)),
        ((3, nz), (nz, NY)),
        ((3,), (nx,)),
        ((nx,), (nx,)),
        ((NY,), (NY,)),
        ((nz,), (nz,)),
        ((n_col,), (n_col,)),
        ((n_col,), (n_col,)),
        ((n_col,), (n_col,)),
    ):
        scratch += [dma(sent), dma(received)]
    scratch.append(dma((6,)))
    run = pl.pallas_call(
        functools.partial(kernel, n_row, n_col, scale),
        out_shape=jax.ShapeDtypeStruct((8, 128), F32),
        in_specs=[hbm, hbm, hbm, hbm, smem, smem],
        out_specs=vmem,
        scratch_shapes=scratch,
        compiler_params=pltpu.CompilerParams(
            collective_id=0, has_side_effects=True, vmem_limit_bytes=56 * 1024 * 1024
        ),
    )
    both = run(
        feat_a,
        feat_b.reshape(width // STRIP, STRIP, ch),
        conv_weight.reshape(3, 3 * ch, desc),
        conv_bias.reshape(1, desc),
        pair_lists.T,
        pair_counts,
    )
    return (both[0:4], both[4:5])


def solution(mesh):
    in_specs = (P("row", "col", None), P("row", "col", None), P(), P(), P(), P())
    out_specs = (P("row", "col"), P("row", "col"))
    return jax.shard_map(local, mesh=mesh, in_specs=in_specs, out_specs=out_specs, check_vma=False)
```
